512 devices in a mesh: row: 16 (over z, core), col: 32 (over y, x).
Axes of the slice: x: 4, y: 8, z: 8, core: 2. Of those that a mesh axis runs over, the one named last changes fastest.
Arguments:
- config: float32 [6, 65536], P(None, ('row', 'col')), as said below
- start: float32 [6, 65536], P(None, ('row', 'col')), may hold values from -6 to 6
- tile_list: int32 [16, 32, 8, 5], P('row', 'col'), may hold values from -1 to 31, as said below
- tile_count: int32 [16, 32], P('row', 'col'), may hold values from 1 to 8, as said below
Outputs:
- coefficients: float32 [4], replicated
- mode: float32 [6, 65536], P(None, ('row', 'col'))
The draws below stay inside these ranges and needn't reach their ends.
Inputs may be any that keep to these rules, and one draw needn't show every extreme that they name: `tile_list`: entry k of device (r, c) is used when k < tile_count[r, c]; its first value is a row tile 0 to 31, its second a column tile 0 to 15, the last three are offsets in -1, 0, 1, not all zero. Unused entries hold values of the same law. `tile_count`: some device uses all 8 entries. `config`: rows 3 to 5 are unit vectors. No two ellipsoids intersect, within a tile or across tiles placed by a list entry's offsets.
All inputs are finite; a program needn't handle non-finite values.
Results may differ from the reference program's by a relative error of at most 0.0003.
Values sent between devices are 32-bit elements; how exact they have to be, the bound alone decides.
A program may use at most 64 MiB of HBM per device.

```python
import math
import jax
import jax.numpy as jnp
from jax import lax

TILE = 128
MAXT = 8
PARTICLES = 65536
N_ROW = 16
N_COL = 32


def draw_config(key, part):
    keys = jax.random.split(jax.random.fold_in(key, 5), 5)
    ordinal = jnp.arange(PARTICLES, dtype=jnp.int32) % TILE
    lattice_x = (ordinal % 4).astype(jnp.float32) * 1.25
    lattice_y = (ordinal // 4 % 4).astype(jnp.float32) * 1.25
    lattice_z = (ordinal // 16).astype(jnp.float32) * 3.5
    shake_xy = jax.random.uniform(keys[0], (2, PARTICLES), jnp.float32, -0.06, 0.06)
    tilt = jax.random.uniform(keys[3], (PARTICLES,), jnp.float32, 0.0, 0.25)
    shake_z = jax.random.uniform(keys[2], (PARTICLES,), jnp.float32, -0.1, 0.1)
    turn = jax.random.uniform(keys[4], (PARTICLES,), jnp.float32, 0.0, 2.0 * math.pi)
    rows = [lattice_x + shake_xy[0], lattice_y + shake_xy[1], lattice_z + shake_z, jnp.sin(tilt) * jnp.cos(turn), jnp.sin(tilt) * jnp.sin(turn), jnp.cos(tilt)]
    return jnp.stack(rows).astype(jnp.float32)


def list_tables(key):
    keys = jax.random.split(jax.random.fold_in(key, 71), 8)
    row_ids = jnp.arange(N_ROW, dtype=jnp.int32)[:, None]
    col_ids = jnp.arange(N_COL, dtype=jnp.int32)[None, :]
    first = jax.random.randint(keys[0], (N_ROW, N_COL, MAXT), 0, N_COL, dtype=jnp.int32)
    second = jax.random.randint(keys[1], (N_ROW, N_COL, MAXT), 0, N_ROW, dtype=jnp.int32)
    rotate_a = jax.random.randint(keys[2], (), 0, N_COL, dtype=jnp.int32)
    rotate_b = jax.random.randint(keys[3], (), 0, N_ROW, dtype=jnp.int32)
    first = first.at[:, :, 0].set((col_ids + row_ids + rotate_a) % N_COL)
    second = second.at[:, :, 0].set((row_ids + col_ids + rotate_b) % N_ROW)
    chosen = jax.random.randint(keys[4], (N_ROW, N_COL, MAXT), 0, 26, dtype=jnp.int32)
    code = chosen + (chosen >= 13).astype(jnp.int32)
    offset_x = code // 9 - 1
    offset_y = code // 3 % 3 - 1
    offset_z = code % 3 - 1
    table = jnp.stack([first, second, offset_x, offset_y, offset_z], axis=-1).astype(jnp.int32)
    factor_a = jax.random.randint(keys[5], (N_ROW * N_COL,), 0, MAXT, dtype=jnp.int32)
    factor_b = jax.random.randint(keys[6], (N_ROW * N_COL,), 0, MAXT, dtype=jnp.int32)
    counts = 1 + factor_a * factor_b // MAXT
    busiest = jax.random.randint(keys[7], (), 0, N_ROW * N_COL, dtype=jnp.int32)
    counts = counts.at[busiest].set(MAXT)
    return (table, counts.reshape(N_ROW, N_COL).astype(jnp.int32))


def draw_tile_list(key, part):
    return list_tables(key)[0]


def draw_tile_count(key, part):
    return list_tables(key)[1]


def level_of(rng, shape, cuts, smallest, largest):
    def one(axis_at, shards_of):
        heights = jax.random.uniform(jax.random.fold_in(jax.random.fold_in(rng, 6), axis_at), (shards_of,), jnp.float32, smallest / len(cuts), largest / len(cuts))
        return jnp.repeat(jnp.exp(heights), shape[axis_at] // shards_of).reshape((-1,) + (1,) * (len(shape) - axis_at - 1))

    loudness = one(*cuts[0])
    for cut in cuts[1:]:
        loudness = loudness * one(*cut)
    return loudness


def bell_draw(key, extent, width, limit, shards=(), kind=jnp.bfloat16):
    drawn = jax.random.normal(key, extent, jnp.float32) * width
    if len(shards) > 0:
        drawn = level_of(key, extent, shards, -0.22, 0.18) * drawn
    return jnp.clip(drawn, min=-limit, max=limit).astype(kind)


def setup_inputs(seed: int = 0) -> dict:
    key_list = jax.random.split(jax.random.key(seed), 5)
    config = draw_config(jax.random.fold_in(key_list[4], 71), 0)
    start = bell_draw(key_list[1], (6, PARTICLES), 1.0, 6.0, ((1, 512),), jnp.float32)
    tile_list = draw_tile_list(jax.random.fold_in(key_list[4], 71), 0)
    tile_count = draw_tile_count(jax.random.fold_in(key_list[4], 71), 0)
    return dict(config=config, start=start, tile_list=tile_list, tile_count=tile_count)


chi_shape = 0.8
chi_energy = (math.sqrt(5.0) - 1.0) / (math.sqrt(5.0) + 1.0)
well_depth = 0.005
cutoff_sq = 20.25
norm_eps = 1e-06

def rotate(heading, turn):
    moved = heading + jnp.cross(turn, heading, axis=0)
    return moved / jnp.sqrt(lax.optimization_barrier(jnp.sum(moved * moved, axis=0, keepdims=True)))

def place(frame, dof):
    return (frame[:3] + dof[:3], rotate(frame[3:], dof[3:]))

def pair_energy(separation, left_axis, right_axis):
    distance_sq = lax.optimization_barrier(jnp.sum(separation * separation, axis=0))
    distance = jnp.sqrt(distance_sq)
    direction = separation / distance
    along_left = lax.optimization_barrier(jnp.sum(direction * left_axis, axis=0))
    along_right = lax.optimization_barrier(jnp.sum(direction * right_axis, axis=0))
    cosine = lax.optimization_barrier(jnp.sum(left_axis * right_axis, axis=0))
    summed_sq = (along_left + along_right) ** 2
    differ_sq = (along_left - along_right) ** 2
    shape_term = 1.0 - 0.5 * chi_shape * (summed_sq / (1.0 + chi_shape * cosine) + differ_sq / (1.0 - chi_shape * cosine))
    contact = 1.0 / jnp.sqrt(shape_term)
    strength_one = 1.0 / jnp.sqrt(1.0 - chi_shape * chi_shape * cosine * cosine)
    strength_two = 1.0 - 0.5 * chi_energy * (summed_sq / (1.0 + chi_energy * cosine) + differ_sq / (1.0 - chi_energy * cosine))
    reduced = 1.0 / (distance - contact + 1.0)
    sixth = reduced ** 6
    switch = jnp.maximum(1.0 - distance_sq / cutoff_sq, 0.0) ** 3
    return 4.0 * well_depth * strength_one * strength_two * strength_two * (sixth * sixth - sixth) * switch

def cross_energy(dof_left, dof_right, left_frame, right_frame, brick_shift):
    left_centre, left_axis = place(left_frame, dof_left)
    right_centre, right_axis = place(right_frame, dof_right)
    separation = right_centre[:, None, :] + brick_shift[:, None, None] - left_centre[:, :, None]
    return jnp.sum(pair_energy(separation, left_axis[:, :, None], right_axis[:, None, :]))

def own_energy(dof, frame):
    centre, heading = place(frame, dof)
    ordinal = lax.iota(jnp.int32, frame.shape[1])
    upper_mask = (ordinal[:, None] < ordinal[None, :]).astype(frame.dtype)
    diagonal = (ordinal[:, None] == ordinal[None, :]).astype(frame.dtype)
    separation = centre[:, None, :] - centre[:, :, None]
    lifted = separation + jnp.stack([0.0 * diagonal, 0.0 * diagonal, 8.0 * diagonal])
    return jnp.sum(upper_mask * pair_energy(lifted, heading[:, :, None], heading[:, None, :]))

def cross_product(left_frame, right_frame, left_tangent, right_tangent, brick_shift):

    def gradient(dof_left, dof_right):
        return jax.grad(cross_energy, argnums=(0, 1))(dof_left, dof_right, left_frame, right_frame, brick_shift)
    anchor = (jnp.zeros_like(left_tangent), jnp.zeros_like(right_tangent))
    _, tangent = jax.jvp(gradient, anchor, (left_tangent, right_tangent))
    return tangent

def own_product(frame, vector):

    def gradient(dof):
        return jax.grad(own_energy)(dof, frame)
    _, tangent = jax.jvp(gradient, (jnp.zeros_like(vector),), (vector,))
    return tangent

def apply_hessian(config, vector, tile_list, tile_count):
    tiles = N_ROW * N_COL
    period = jnp.array([5.0, 5.0, 3.5 * (TILE // 16)], dtype=config.dtype)
    frames = config.reshape(6, tiles, TILE).transpose(1, 0, 2)
    pieces = vector.reshape(6, tiles, TILE).transpose(1, 0, 2)
    own_terms = lax.map(lambda both: own_product(both[0], both[1]), (frames, pieces))
    result = own_terms.transpose(1, 0, 2).reshape(6, tiles * TILE)
    entries = tile_list.reshape(tiles * MAXT, 5)
    ordinal = jnp.arange(tiles * MAXT, dtype=jnp.int32)
    row_of = ordinal // (N_COL * MAXT)
    col_of = ordinal // MAXT % N_COL
    active = ordinal % MAXT < tile_count.reshape(tiles)[ordinal // MAXT]

    def visit(total, item):
        entry, row_id, col_id, flag = item
        left = ((row_id * N_COL + entry[0]) * TILE).astype(jnp.int32)
        right = ((entry[1] * N_COL + col_id) * TILE).astype(jnp.int32)
        brick_shift = entry[2:5].astype(config.dtype) * period

        def compute(marker):
            return cross_product(lax.dynamic_slice_in_dim(config, left, TILE, 1), lax.dynamic_slice_in_dim(config, right, TILE, 1), lax.dynamic_slice_in_dim(vector, left, TILE, 1), lax.dynamic_slice_in_dim(vector, right, TILE, 1), brick_shift)

        def skip(marker):
            return (jnp.zeros((6, TILE), total.dtype), jnp.zeros((6, TILE), total.dtype))
        left_out, right_out = lax.cond(flag, compute, skip, flag)
        total = lax.dynamic_update_slice_in_dim(total, lax.dynamic_slice_in_dim(total, left, TILE, 1) + left_out, left, 1)
        total = lax.dynamic_update_slice_in_dim(total, lax.dynamic_slice_in_dim(total, right, TILE, 1) + right_out, right, 1)
        return (total, None)
    result, _ = lax.scan(visit, result, (entries, row_of, col_of, active))
    return result

def reference(config, start, tile_list, tile_count):
    total_entries = 6 * PARTICLES

    def mean_of(values):
        return jnp.sum(values) / total_entries
    first = start / jnp.sqrt(mean_of(start * start) + norm_eps)
    image = apply_hessian(config, first, tile_list, tile_count)
    alpha_one = mean_of(first * image)
    image = image - alpha_one * first
    beta_one = jnp.sqrt(mean_of(image * image) + norm_eps)
    second = image / beta_one
    image = apply_hessian(config, second, tile_list, tile_count) - beta_one * first
    alpha_two = mean_of(second * image)
    image = image - alpha_two * second
    beta_two = jnp.sqrt(mean_of(image * image) + norm_eps)
    mode = image / beta_two
    return (jnp.stack([alpha_one, beta_one, alpha_two, beta_two]), mode)
```

```python
import functools
import math

import jax
import jax.numpy as jnp
from jax import lax
from jax.experimental import pallas as pl
from jax.experimental.pallas import tpu as pltpu
from jax.sharding import PartitionSpec as P

MESH = pl.DeviceIdType.MESH
chi_shape = 0.8
chi_energy = (math.sqrt(5.0) - 1.0) / (math.sqrt(5.0) + 1.0)
well_depth = 0.005
cutoff_sq = 20.25
norm_eps = 1e-06
LANES = 128
CHUNK = 8
KEPT = 20


def dot3(a, b):
    return a[0] * b[0] + a[1] * b[1] + a[2] * b[2]


def cross3(a, b):
    return (
        a[1] * b[2] - a[2] * b[1],
        a[2] * b[0] - a[0] * b[2],
        a[0] * b[1] - a[1] * b[0],
    )


def anisotropy(x, spread, tau, A, B, c, norm, twice_cab, prod_tau):
    t = (2.0 * x) * spread * tau
    h = 0.5 * t * (norm - x * twice_cab)
    xc = x * c
    gA = t * (xc * B - A)
    gB = t * (xc * A - B)
    e = (2.0 * x * x) * spread
    gc = e * (prod_tau - c * h)
    gAB = xc * t
    gAc = e * (c * gA + B * tau)
    gBc = e * (c * gB + A * tau)
    gcc = e * (2.0 * c * gc - h)
    tau2 = 2.0 * tau
    gx = tau2 * h
    first = (gx, gA, gB, gc)
    second = {
        (0, 0): -2.0 * tau2 * gx,
        (0, 1): -tau2 * gA,
        (0, 2): -tau2 * gB,
        (0, 3): -tau2 * gc,
        (1, 1): -t,
        (1, 2): gAB,
        (1, 3): gAc,
        (2, 2): -t,
        (2, 3): gBc,
        (3, 3): gcc,
    }
    return 1.0 - h, first, second


PAIRS = [(p, q) for p in range(4) for q in range(p, 4)]


def derivatives(rho, A, B, c):
    kappa = 1.0 / cutoff_sq
    inv_r = lax.rsqrt(rho)
    tau = inv_r * inv_r
    cc = c * c
    e1 = lax.rsqrt(1.0 - (chi_shape * chi_shape) * cc)
    D1 = e1 * e1
    D2 = 1.0 / (1.0 - (chi_energy * chi_energy) * cc)
    AB = A * B
    norm = A * A + B * B
    twice_cab = 2.0 * c * AB
    prod_tau = AB * tau
    g, g1, g2 = anisotropy(chi_shape, D1, tau, A, B, c, norm, twice_cab, prod_tau)
    q, q1, q2 = anisotropy(chi_energy, D2, tau, A, B, c, norm, twice_cab, prod_tau)
    sigma = lax.rsqrt(g)
    root_g = g * sigma
    alpha = 0.5 * sigma * sigma * sigma
    s = 1.0 / (rho * inv_r - sigma + 1.0)
    s2 = s * s
    s6 = s2 * s2 * s2
    p = jnp.maximum(1.0 - kappa * rho, 0.0)
    inv_p = jnp.where(p > 0.0, 1.0 / p, 0.0)
    weight = (4.0 * well_depth) * e1 * (q * q) * (p * p * p) * s6
    w0 = weight * (s6 - 1.0)
    w1 = weight * s * (6.0 - 12.0 * s6)
    w2 = weight * s2 * (156.0 * s6 - 42.0)
    twice_inv_q = 2.0 / q
    L = [twice_inv_q * f for f in q1]
    lP = (-6.0 * kappa) * inv_p
    lK = (chi_shape * chi_shape) * c * D1
    lKK = (chi_shape * chi_shape) * D1 * (2.0 * D1 - 1.0)
    l = [L[0] + lP, L[1], L[2], L[3] + lK]
    G = [alpha * f for f in g1]
    R = [G[0] + inv_r, G[1], G[2], G[3]]
    half = [0.5 * f for f in L]
    bend = [3.0 * root_g * f for f in G]
    up = [w0 * l[k] + w1 * R[k] for k in range(4)]
    tp = [w1 * l[k] + w2 * R[k] for k in range(4)]
    w1a = w1 * alpha
    w0q = w0 * twice_inv_q
    out = []
    for a, b in PAIRS:
        value = up[a] * l[b] + tp[a] * R[b]
        value = value + w0q * q2[(a, b)] - w0 * (half[a] * L[b])
        value = value + w1a * g2[(a, b)] - w1 * (bend[a] * G[b])
        if (a, b) == (0, 0):
            value = value - w0 * (lP * lP) * (1.0 / 3.0) - w1 * (inv_r * tau)
        if (a, b) == (3, 3):
            value = value + w0 * lKK
        out.append(value)
    return up, out


def apply_pairs(d, u, v, dd, m, n, F, FF):
    S = dict(zip(PAIRS, FF))
    delta = (
        dot3(d, dd),
        dot3(u, dd) + dot3(d, m),
        dot3(v, dd) + dot3(d, n),
        dot3(v, m) + dot3(u, n),
    )
    dF = []
    for p in range(4):
        terms = [S[(min(p, q), max(p, q))] * delta[q] for q in range(4)]
        dF.append((terms[0] + terms[1]) + (terms[2] + terms[3]))
    Gd, Gu, Gv = [], [], []
    for k in range(3):
        Gd.append(
            (dF[0] * d[k] + F[0] * dd[k])
            + (dF[1] * u[k] + F[1] * m[k])
            + (dF[2] * v[k] + F[2] * n[k])
        )
        Gu.append((dF[1] * d[k] + F[1] * dd[k]) + (dF[3] * v[k] + F[3] * n[k]))
        Gv.append((dF[2] * d[k] + F[2] * dd[k]) + (dF[3] * u[k] + F[3] * m[k]))
    return Gd, Gu, Gv


def full(row):
    return jnp.broadcast_to(row, (CHUNK, LANES))


def rows_of(frame, vector):
    c = [frame[k : k + 1, :] for k in range(3)]
    u = [frame[3 + k : 4 + k, :] for k in range(3)]
    y = [vector[k : k + 1, :] for k in range(3)]
    w = [vector[3 + k : 4 + k, :] for k in range(3)]
    return c, u, y, list(cross3(w, u))


def put_columns(cols_ref, rows):
    pad = 16 - len(rows)
    block = jnp.concatenate(list(rows) + [jnp.zeros((pad, LANES), jnp.float32)], axis=0)
    cols_ref[...] = block.T


def gather_sums(sums_ref):
    return sums_ref[...].T


def column(block, p):
    return jnp.broadcast_to(block[:, p : p + 1], (CHUNK, LANES))


def merge_columns(values):
    lane = lax.broadcasted_iota(jnp.int32, (CHUNK, LANES), 1)
    out = jnp.zeros((CHUNK, LANES), jnp.float32)
    for k, value in enumerate(values):
        out = jnp.where(lane == k, jnp.sum(value, axis=1, keepdims=True), out)
    return out


def first_pass(slot, left, right, shift, cols_ref, sums_ref, kept_ref, own):
    cl, ul, yl, ml = left
    cr, ur, yr, nr = right
    put_columns(cols_ref, cl + ul + yl + ml)
    c_right = [full(cr[k] + shift[k]) for k in range(3)]
    v = [full(f) for f in ur]
    y_right = [full(f) for f in yr]
    n = [full(f) for f in nr]
    lane = lax.broadcasted_iota(jnp.int32, (CHUNK, LANES), 1)
    sub = lax.broadcasted_iota(jnp.int32, (CHUNK, LANES), 0)

    def chunk(i, acc):
        at = pl.multiple_of(i * CHUNK, CHUNK)
        block = cols_ref[pl.ds(at, CHUNK), :]
        d = [c_right[k] - column(block, k) for k in range(3)]
        u = [column(block, 3 + k) for k in range(3)]
        dd = [y_right[k] - column(block, 6 + k) for k in range(3)]
        m = [column(block, 9 + k) for k in range(3)]
        if own:
            d[2] = d[2] + jnp.where(sub + at == lane, 8.0, 0.0)
        A, B, c = dot3(d, u), dot3(d, v), dot3(u, v)
        F, FF = derivatives(dot3(d, d), A, B, c)
        if own:
            upper = sub + at < lane
            F = [jnp.where(upper, f, 0.0) for f in F]
            FF = [jnp.where(upper, f, 0.0) for f in FF]
        for k, value in enumerate(d + u + F + FF):
            kept_ref[slot, k, pl.ds(at, CHUNK), :] = value
        Gd, Gu, Gv = apply_pairs(d, u, v, dd, m, n, F, FF)
        fc = F[3] * c
        sums_ref[pl.ds(at, CHUNK), :] = merge_columns(Gd + Gu + [F[1] * A + fc])
        return tuple(a + g for a, g in zip(acc, Gd + Gv + [F[2] * B + fc]))

    zero = jnp.zeros((CHUNK, LANES), jnp.float32)
    acc = lax.fori_loop(0, LANES // CHUNK, chunk, (zero,) * 7)
    left_sums = gather_sums(sums_ref)
    left_curve = left_sums[6:7, :]
    right_rows = [jnp.sum(a, axis=0, keepdims=True) for a in acc]
    left_out, right_out = finish(left_sums, right_rows, left_curve, right_rows[6], ml, nr)
    return left_out, right_out, left_curve, right_rows[6]


def second_pass(slot, left, right, cols_ref, sums_ref, kept_ref, left_curve, right_curve):
    _, _, yl, ml = left
    _, ur, yr, nr = right
    put_columns(cols_ref, yl + ml)
    v = [full(f) for f in ur]
    y_right = [full(f) for f in yr]
    n = [full(f) for f in nr]

    def chunk(i, acc):
        at = pl.multiple_of(i * CHUNK, CHUNK)
        block = cols_ref[pl.ds(at, CHUNK), :]
        kept = [kept_ref[slot, k, pl.ds(at, CHUNK), :] for k in range(KEPT)]
        dd = [y_right[k] - column(block, k) for k in range(3)]
        m = [column(block, 3 + k) for k in range(3)]
        Gd, Gu, Gv = apply_pairs(kept[0:3], kept[3:6], v, dd, m, n, kept[6:10], kept[10:20])
        sums_ref[pl.ds(at, CHUNK), :] = merge_columns(Gd + Gu)
        return tuple(a + g for a, g in zip(acc, Gd + Gv))

    zero = jnp.zeros((CHUNK, LANES), jnp.float32)
    acc = lax.fori_loop(0, LANES // CHUNK, chunk, (zero,) * 6)
    left_sums = gather_sums(sums_ref)
    right_rows = [jnp.sum(a, axis=0, keepdims=True) for a in acc]
    return finish(left_sums, right_rows, left_curve, right_curve, ml, nr)


def finish(left_sums, right_rows, left_curve, right_curve, ml, nr):
    blank = jnp.zeros((2, LANES), jnp.float32)
    left_out = jnp.concatenate(
        [-left_sums[k : k + 1, :] for k in range(3)]
        + [left_sums[3 + k : 4 + k, :] - left_curve * ml[k] for k in range(3)]
        + [blank],
        axis=0,
    )
    right_out = jnp.concatenate(
        right_rows[0:3]
        + [right_rows[3 + k] - right_curve * nr[k] for k in range(3)]
        + [blank],
        axis=0,
    )
    return left_out, right_out


def triple_of(x, z):
    F = jnp.sum(x * x, axis=0, keepdims=True)
    some = F > 0.0
    a = jnp.where(some, jnp.sum(x * z, axis=0, keepdims=True) / jnp.where(some, F, 1.0), 0.0)
    rest = z - a * x
    return F, a, jnp.sum(rest * rest, axis=0, keepdims=True)


def merge_triples(F, a, R, axis):
    total = jnp.sum(F, axis=axis, keepdims=True)
    some = total > 0.0
    mean = jnp.where(some, jnp.sum(F * a, axis=axis, keepdims=True) / jnp.where(some, total, 1.0), 0.0)
    gap = a - mean
    return total, mean, jnp.sum(R + F * (gap * gap), axis=axis, keepdims=True)


def pack_triple(triple):
    return jnp.concatenate(list(triple) + [jnp.zeros((5, LANES), jnp.float32)], axis=0)


def unpack_triples(block):
    return block[:, 0, :], block[:, 1, :], block[:, 2, :]


def kernel(
    n_row, n_col,
    frame_ref, start_ref, list_ref, count_ref,
    coef_ref, mode_ref,
    row_frames, col_frames, row_starts, col_starts, row_images, col_images,
    row_in, col_in, row_in2, col_in2, row_out, col_out,
    tri_row, tri_col, tri_row2, tri_col2, tri_buf,
    image_buf, left_outs, right_outs, curves, kept_ref, cols_ref, sums_ref,
    send_sem, recv_sem,
):
    entries = list_ref.shape[0]
    r = lax.axis_index("row")
    c = lax.axis_index("col")
    total_entries = float(6 * LANES * n_row * n_col)
    zero3 = (0.0, 0.0, 0.0)

    def peer_col(k):
        return lax.rem(c + k, n_col)

    def peer_row(k):
        return lax.rem(r + k, n_row)

    def send(src, dst, phase, lane, device):
        pltpu.make_async_remote_copy(
            src_ref=src,
            dst_ref=dst,
            send_sem=send_sem.at[phase, lane],
            recv_sem=recv_sem.at[phase, lane],
            device_id=device,
            device_id_type=MESH,
        ).start()

    def all_wait(buf, n, sem):
        view = buf.at[pl.ds(0, n - 1)]
        pltpu.make_async_copy(view, view, sem).wait()

    barrier = pltpu.get_barrier_semaphore()

    @pl.loop(1, n_col)
    def _(k):
        pl.semaphore_signal(barrier, inc=1, device_id={"col": peer_col(k)}, device_id_type=MESH)

    @pl.loop(1, n_row)
    def _(k):
        pl.semaphore_signal(barrier, inc=1, device_id={"row": peer_row(k)}, device_id_type=MESH)

    frame = frame_ref[...]
    start = start_ref[...]
    mine = rows_of(frame, start)
    own1, own2, lc, rc = first_pass(entries, mine, mine, zero3, cols_ref, sums_ref, kept_ref, True)
    curves[entries, 0:1, :] = lc
    curves[entries, 1:2, :] = rc
    own_first = own1 + own2

    pl.semaphore_wait(barrier, n_row + n_col - 2)

    def spread(row_src, row_buf, col_src, col_buf, phase):
        @pl.loop(1, n_col)
        def _(k):
            send(row_src, row_buf.at[c], phase, 0, {"col": peer_col(k)})

        @pl.loop(1, n_row)
        def _(k):
            send(col_src, col_buf.at[r], phase, 1, {"row": peer_row(k)})

    spread(frame_ref, row_frames, frame_ref, col_frames, 0)
    spread(start_ref, row_starts, start_ref, col_starts, 1)
    row_frames[c] = frame
    col_frames[r] = frame
    row_starts[c] = start
    col_starts[r] = start
    all_wait(row_frames, n_col, recv_sem.at[0, 0])
    all_wait(col_frames, n_row, recv_sem.at[0, 1])
    all_wait(row_starts, n_col, recv_sem.at[1, 0])
    all_wait(col_starts, n_row, recv_sem.at[1, 1])

    period = (5.0, 5.0, 3.5 * (LANES // 16))

    def entry_rows(k, row_vectors, col_vectors):
        a = list_ref[k, 0]
        b = list_ref[k, 1]
        left = rows_of(row_frames[a], row_vectors[a])
        right = rows_of(col_frames[b], col_vectors[b])
        return left, right

    @pl.loop(0, entries)
    def _(k):
        left, right = entry_rows(k, row_starts, col_starts)
        shift = [list_ref[k, 2 + x].astype(jnp.float32) * period[x] for x in range(3)]
        lo, ro, lc, rc = first_pass(k, left, right, shift, cols_ref, sums_ref, kept_ref, False)
        left_outs[k] = lo
        right_outs[k] = ro
        curves[k, 0:1, :] = lc
        curves[k, 1:2, :] = rc

    used = count_ref[0, 0]

    def scatter(row_buf, col_buf, phase, own):
        lefts = [jnp.where(k < used, left_outs[k], 0.0) for k in range(entries)]
        rights = [jnp.where(k < used, right_outs[k], 0.0) for k in range(entries)]

        @pl.loop(0, n_col)
        def _(t):
            acc = jnp.zeros((8, LANES), jnp.float32)
            for k in range(entries):
                acc = acc + jnp.where(list_ref[k, 0] == t, lefts[k], 0.0)
            row_out[phase, t] = acc

        @pl.loop(0, n_row)
        def _(t):
            acc = jnp.zeros((8, LANES), jnp.float32)
            for k in range(entries):
                acc = acc + jnp.where(list_ref[k, 1] == t, rights[k], 0.0)
            col_out[phase, t] = acc

        @pl.loop(1, n_col)
        def _(k):
            t = peer_col(k)
            send(row_out.at[phase, t], row_buf.at[c], 2 + phase, 0, {"col": t})

        @pl.loop(1, n_row)
        def _(k):
            t = peer_row(k)
            send(col_out.at[phase, t], col_buf.at[r], 2 + phase, 1, {"row": t})

        row_buf[c] = row_out[phase, c]
        col_buf[r] = col_out[phase, r]
        all_wait(row_buf, n_col, recv_sem.at[2 + phase, 0])
        all_wait(col_buf, n_row, recv_sem.at[2 + phase, 1])
        total = own + jnp.sum(row_buf[...], axis=0) + jnp.sum(col_buf[...], axis=0)
        u = [frame[3 + k : 4 + k, :] for k in range(3)]
        turn = cross3(u, [total[3 + k : 4 + k, :] for k in range(3)])
        return jnp.concatenate([total[0:3, :]] + list(turn), axis=0)

    image = scatter(row_in, col_in, 0, own_first)

    image_buf[...] = image
    spread(image_buf, row_images, image_buf, col_images, 4)
    row_images[c] = image
    col_images[r] = image

    def scalars_out(triple, slot, buf, phase):
        tri_buf[slot] = pack_triple(triple)

        @pl.loop(1, n_row)
        def _(k):
            send(tri_buf.at[slot], buf.at[r], phase, 1, {"row": peer_row(k)})

        buf[r] = tri_buf[slot]

    def scalars_across(buf, slot, buf2, phase):
        all_wait(buf, n_row, recv_sem.at[phase, 1])
        triple = merge_triples(*unpack_triples(buf[...]), 0)
        tri_buf[slot] = pack_triple(triple)

        @pl.loop(1, n_col)
        def _(k):
            send(tri_buf.at[slot], buf2.at[c], phase, 0, {"col": peer_col(k)})

        buf2[c] = tri_buf[slot]

    def scalars_in(buf2, phase):
        all_wait(buf2, n_col, recv_sem.at[phase, 0])
        triple = merge_triples(*unpack_triples(buf2[...]), 0)
        return merge_triples(*triple, 1)

    scalars_out(triple_of(start, image), 0, tri_row, 5)

    mine = rows_of(frame, image)
    own1, own2 = second_pass(
        entries, mine, mine, cols_ref, sums_ref, kept_ref,
        curves[entries, 0:1, :], curves[entries, 1:2, :],
    )
    own_second = own1 + own2

    scalars_across(tri_row, 1, tri_col, 5)
    all_wait(row_images, n_col, recv_sem.at[4, 0])
    all_wait(col_images, n_row, recv_sem.at[4, 1])

    @pl.loop(0, entries)
    def _(k):
        left, right = entry_rows(k, row_images, col_images)
        lo, ro = second_pass(
            k, left, right, cols_ref, sums_ref, kept_ref, curves[k, 0:1, :], curves[k, 1:2, :]
        )
        left_outs[k] = lo
        right_outs[k] = ro

    image2 = scatter(row_in2, col_in2, 1, own_second)

    F, a, R = scalars_in(tri_col, 5)
    inv_n0 = lax.rsqrt(F / total_entries + norm_eps)
    alpha1 = (a * F) * (inv_n0 * inv_n0) / total_entries
    gap = a - alpha1
    beta1 = jnp.sqrt((R + gap * gap * F) * (inv_n0 * inv_n0) / total_entries + norm_eps)
    scale = inv_n0 / beta1
    second = (image - alpha1 * start) * scale
    image3 = (image2 - alpha1 * image) * scale - (beta1 * inv_n0) * start

    scalars_out(triple_of(second, image3), 2, tri_row2, 6)
    scalars_across(tri_row2, 3, tri_col2, 6)
    F, a, R = scalars_in(tri_col2, 6)
    alpha2 = (a * F) / total_entries
    gap = a - alpha2
    beta2 = jnp.sqrt((R + gap * gap * F) / total_entries + norm_eps)
    mode_ref[...] = (image3 - alpha2 * second) / beta2
    coef_ref[0] = alpha1[0, 0]
    coef_ref[1] = beta1[0, 0]
    coef_ref[2] = alpha2[0, 0]
    coef_ref[3] = beta2[0, 0]

    for phase, row_buf, col_buf in (
        (0, row_frames, col_frames),
        (1, row_starts, col_starts),
        (2, row_in, col_in),
        (3, row_in2, col_in2),
        (4, row_images, col_images),
        (5, tri_col, tri_row),
        (6, tri_col2, tri_row2),
    ):
        all_wait(row_buf, n_col, send_sem.at[phase, 0])
        all_wait(col_buf, n_row, send_sem.at[phase, 1])


def solution(mesh):
    n_row, n_col = mesh.shape["row"], mesh.shape["col"]

    def local(config, start, tile_list, tile_count):
        entries = tile_list.shape[2]
        f32 = jnp.float32

        def vm(*shape):
            return pltpu.VMEM(shape, f32)

        scratch = [
            vm(n_col, 6, LANES), vm(n_row, 6, LANES),
            vm(n_col, 6, LANES), vm(n_row, 6, LANES),
            vm(n_col, 6, LANES), vm(n_row, 6, LANES),
            vm(n_col, 8, LANES), vm(n_row, 8, LANES),
            vm(n_col, 8, LANES), vm(n_row, 8, LANES),
            vm(2, n_col, 8, LANES), vm(2, n_row, 8, LANES),
            vm(n_row, 8, LANES), vm(n_col, 8, LANES),
            vm(n_row, 8, LANES), vm(n_col, 8, LANES),
            vm(4, 8, LANES),
            vm(6, LANES),
            vm(entries, 8, LANES), vm(entries, 8, LANES),
            vm(entries + 1, 8, LANES),
            vm(entries + 1, KEPT, LANES, LANES),
            vm(LANES, 16),
            vm(LANES, LANES),
            pltpu.SemaphoreType.DMA((7, 2)),
            pltpu.SemaphoreType.DMA((7, 2)),
        ]
        return pl.pallas_call(
            functools.partial(kernel, n_row, n_col),
            out_shape=(
                jax.ShapeDtypeStruct((4,), f32),
                jax.ShapeDtypeStruct((6, LANES), f32),
            ),
            in_specs=[
                pl.BlockSpec(memory_space=pltpu.VMEM),
                pl.BlockSpec(memory_space=pltpu.VMEM),
                pl.BlockSpec(memory_space=pltpu.SMEM),
                pl.BlockSpec(memory_space=pltpu.SMEM),
            ],
            out_specs=(
                pl.BlockSpec(memory_space=pltpu.SMEM),
                pl.BlockSpec(memory_space=pltpu.VMEM),
            ),
            scratch_shapes=scratch,
            compiler_params=pltpu.CompilerParams(collective_id=0, has_side_effects=True),
        )(config, start, tile_list.reshape(entries, 5), tile_count)

    placed = (
        P(None, ("row", "col")),
        P(None, ("row", "col")),
        P("row", "col", None, None),
        P("row", "col"),
    )
    return jax.shard_map(
        local, mesh=mesh, in_specs=placed, out_specs=(P(), P(None, ("row", "col"))), check_vma=False
    )
```

```python
import functools
import math

import jax
import jax.numpy as jnp
from jax import lax
from jax.experimental import pallas as pl
from jax.experimental.pallas import tpu as pltpu
from jax.sharding import PartitionSpec as P

MESH = pl.DeviceIdType.MESH
chi_shape = 0.8
chi_energy = (math.sqrt(5.0) - 1.0) / (math.sqrt(5.0) + 1.0)
well_depth = 0.005
cutoff_sq = 20.25
norm_eps = 1e-06
LANES = 128
CHUNK = 8
KEPT = 20
UNROLL_FIRST = 4
UNROLL_SECOND = 4


def dot3(a, b):
    return a[0] * b[0] + a[1] * b[1] + a[2] * b[2]


def cross3(a, b):
    return (
        a[1] * b[2] - a[2] * b[1],
        a[2] * b[0] - a[0] * b[2],
        a[0] * b[1] - a[1] * b[0],
    )


def anisotropy(x, spread, tau, A, B, c, norm, twice_cab, prod_tau):
    t = (2.0 * x) * spread * tau
    h = 0.5 * t * (norm - x * twice_cab)
    xc = x * c
    gA = t * (xc * B - A)
    gB = t * (xc * A - B)
    e = (2.0 * x * x) * spread
    gc = e * (prod_tau - c * h)
    gAB = xc * t
    gAc = e * (c * gA + B * tau)
    gBc = e * (c * gB + A * tau)
    gcc = e * (2.0 * c * gc - h)
    tau2 = 2.0 * tau
    gx = tau2 * h
    first = (gx, gA, gB, gc)
    second = {
        (0, 0): -2.0 * tau2 * gx,
        (0, 1): -tau2 * gA,
        (0, 2): -tau2 * gB,
        (0, 3): -tau2 * gc,
        (1, 1): -t,
        (1, 2): gAB,
        (1, 3): gAc,
        (2, 2): -t,
        (2, 3): gBc,
        (3, 3): gcc,
    }
    return 1.0 - h, first, second


PAIRS = [(p, q) for p in range(4) for q in range(p, 4)]


def derivatives(rho, A, B, c):
    kappa = 1.0 / cutoff_sq
    inv_r = lax.rsqrt(rho)
    tau = inv_r * inv_r
    cc = c * c
    e1 = lax.rsqrt(1.0 - (chi_shape * chi_shape) * cc)
    D1 = e1 * e1
    D2 = 1.0 / (1.0 - (chi_energy * chi_energy) * cc)
    AB = A * B
    norm = A * A + B * B
    twice_cab = 2.0 * c * AB
    prod_tau = AB * tau
    g, g1, g2 = anisotropy(chi_shape, D1, tau, A, B, c, norm, twice_cab, prod_tau)
    q, q1, q2 = anisotropy(chi_energy, D2, tau, A, B, c, norm, twice_cab, prod_tau)
    sigma = lax.rsqrt(g)
    root_g = g * sigma
    alpha = 0.5 * sigma * sigma * sigma
    s = 1.0 / (rho * inv_r - sigma + 1.0)
    s2 = s * s
    s6 = s2 * s2 * s2
    p = jnp.maximum(1.0 - kappa * rho, 0.0)
    inv_p = jnp.where(p > 0.0, 1.0 / p, 0.0)
    weight = (4.0 * well_depth) * e1 * (q * q) * (p * p * p) * s6
    w0 = weight * (s6 - 1.0)
    w1 = weight * s * (6.0 - 12.0 * s6)
    w2 = weight * s2 * (156.0 * s6 - 42.0)
    twice_inv_q = 2.0 / q
    L = [twice_inv_q * f for f in q1]
    lP = (-6.0 * kappa) * inv_p
    lK = (chi_shape * chi_shape) * c * D1
    lKK = (chi_shape * chi_shape) * D1 * (2.0 * D1 - 1.0)
    l = [L[0] + lP, L[1], L[2], L[3] + lK]
    G = [alpha * f for f in g1]
    R = [G[0] + inv_r, G[1], G[2], G[3]]
    up = [w0 * l[k] + w1 * R[k] for k in range(4)]
    tp = [w1 * l[k] + w2 * R[k] for k in range(4)]
    w0h = 0.5 * w0
    w1b = (3.0 * root_g) * w1
    upp = [up[k] - w0h * L[k] for k in range(4)]
    tpp = [tp[k] - w1b * G[k] for k in range(4)]
    w1a = w1 * alpha
    w0q = w0 * twice_inv_q
    out = []
    for a, b in PAIRS:
        value = (upp[a] * L[b] + tpp[a] * G[b]) + (w0q * q2[(a, b)] + w1a * g2[(a, b)])
        if b == 3:
            value = value + up[a] * lK
        if (a, b) == (0, 0):
            value = value + (up[0] - w0 * lP * (1.0 / 3.0)) * lP + (tp[0] - w1 * tau) * inv_r
        if (a, b) == (3, 3):
            value = value + w0 * lKK
        out.append(value)
    return up, out


def apply_pairs(d, u, v, dd, m, n, F, FF):
    S = dict(zip(PAIRS, FF))
    delta = (
        dot3(d, dd),
        dot3(u, dd) + dot3(d, m),
        dot3(v, dd) + dot3(d, n),
        dot3(v, m) + dot3(u, n),
    )
    dF = []
    for p in range(4):
        terms = [S[(min(p, q), max(p, q))] * delta[q] for q in range(4)]
        dF.append((terms[0] + terms[1]) + (terms[2] + terms[3]))
    Gd, Gu, Gv = [], [], []
    for k in range(3):
        Gd.append(
            (dF[0] * d[k] + F[0] * dd[k])
            + (dF[1] * u[k] + F[1] * m[k])
            + (dF[2] * v[k] + F[2] * n[k])
        )
        Gu.append((dF[1] * d[k] + F[1] * dd[k]) + (dF[3] * v[k] + F[3] * n[k]))
        Gv.append((dF[2] * d[k] + F[2] * dd[k]) + (dF[3] * u[k] + F[3] * m[k]))
    return Gd, Gu, Gv


def full(row):
    return jnp.broadcast_to(row, (CHUNK, LANES))


def skew(row):
    return pltpu.roll(full(row), 0, 1, stride=1, stride_axis=0)


def unskew_sum(a):
    for rows in (4, 2, 1):
        a = a[0:rows, :] + pltpu.roll(a[rows : 2 * rows, :], LANES - rows, 1)
    return a


def rows_of(frame, vector):
    c = [frame[k : k + 1, :] for k in range(3)]
    u = [frame[3 + k : 4 + k, :] for k in range(3)]
    y = [vector[k : k + 1, :] for k in range(3)]
    w = [vector[3 + k : 4 + k, :] for k in range(3)]
    return c, u, y, list(cross3(w, u))


def place_tile(slot, left, right, shift, bufs):
    left_ref, right_ref = bufs[0], bufs[1]
    cl, ul, yl, ml = left
    cr, ur, yr, nr = right
    if shift is not None:
        for k in range(3):
            left_ref[slot, k] = full(cl[k])
            left_ref[slot, 3 + k] = full(ul[k])
            right_ref[slot, 6 + k] = skew(cr[k] + shift[k])
            right_ref[slot, 9 + k] = skew(ur[k])
    for k in range(3):
        left_ref[slot, 6 + k] = full(yl[k])
        left_ref[slot, 9 + k] = full(ml[k])
        right_ref[slot, k] = skew(yr[k])
        right_ref[slot, 3 + k] = skew(nr[k])


def sweep(step, bufs, slot0, slots, unroll, turned, width):
    _, right_ref, turn_ref, raw_ref, left_sums, right_sums, _ = bufs
    chunks = LANES // CHUNK
    groups = chunks // unroll

    def turn_rows(trip):
        slot = slot0 + trip // groups
        side = lax.rem(trip, 2)
        for s in range(unroll):
            by = (lax.rem(trip, groups) * unroll + s) * CHUNK
            for k in range(turned):
                turn_ref[side, s, k] = pltpu.roll(right_ref[slot, k], by, 1)

    def turn_back(trip):
        slot = slot0 + trip // groups
        group = lax.rem(trip, groups)
        side = lax.rem(trip, 2)
        for k in range(width):
            total = None
            for s in range(unroll):
                by = lax.rem(LANES - (group * unroll + s) * CHUNK, LANES)
                part = pltpu.roll(raw_ref[side, s, k], by, 1)
                total = part if total is None else total + part
            right_sums[slot, group, k] = total

    def body(trip):
        slot = slot0 + trip // groups
        group = lax.rem(trip, groups)
        side = lax.rem(trip, 2)
        sums = None
        for s in range(unroll):
            left_terms, right_terms = step(slot, group * unroll + s, side, s)
            for k in range(width):
                raw_ref[side, s, k] = right_terms[k]
            sums = left_terms if sums is None else [a + b for a, b in zip(sums, left_terms)]
        for k in range(width):
            left_sums[slot, group, k] = sums[k]

    trips = slots * groups
    turn_rows(0)

    def first(trip, carry):
        turn_rows(trip + 1)
        body(trip)
        return carry

    def later(trip, carry):
        turn_back(trip - 1)
        turn_rows(trip + 1)
        body(trip)
        return carry

    first(0, 0)
    lax.fori_loop(1, trips - 1, later, 0)
    turn_back(trips - 2)
    body(trips - 1)
    turn_back(trips - 1)


def collect(slot, bufs, groups, width):
    left_sums, right_sums = bufs[4], bufs[5]
    left, right = [], []
    for k in range(width):
        a, b = left_sums[slot, 0, k], right_sums[slot, 0, k]
        for g in range(1, groups):
            a = a + left_sums[slot, g, k]
            b = b + right_sums[slot, g, k]
        left.append(jnp.sum(a, axis=0, keepdims=True))
        right.append(unskew_sum(b))
    return left, right


def first_sweep(bufs, slot0, slots, own):
    left_ref, _, turn_ref, _, _, _, kept_ref = bufs
    lane = lax.broadcasted_iota(jnp.int32, (CHUNK, LANES), 1)
    sub = lax.broadcasted_iota(jnp.int32, (CHUNK, LANES), 0)

    def step(slot, t, side, s):
        left = [left_ref[slot, k] for k in range(12)]
        right = [turn_ref[side, s, k] for k in range(12)]
        d = [right[6 + k] - left[k] for k in range(3)]
        u, v = left[3:6], right[9:12]
        dd = [right[k] - left[6 + k] for k in range(3)]
        m, n = left[9:12], right[3:6]
        if own:
            gap = sub + t * CHUNK
            d[2] = d[2] + jnp.where(gap == 0, 8.0, 0.0)
        A, B, c = dot3(d, u), dot3(d, v), dot3(u, v)
        F, FF = derivatives(dot3(d, d), A, B, c)
        if own:
            once = (gap > 0) & (lane >= gap)
            F = [jnp.where(once, f, 0.0) for f in F]
            FF = [jnp.where(once, f, 0.0) for f in FF]
        for k, value in enumerate(d + v + F + FF):
            kept_ref[slot, t, k] = value
        Gd, Gu, Gv = apply_pairs(d, u, v, dd, m, n, F, FF)
        fc = F[3] * c
        return Gd + Gu + [F[1] * A + fc], Gd + Gv + [F[2] * B + fc]

    sweep(step, bufs, slot0, slots, UNROLL_FIRST, 12, 7)


def second_sweep(bufs, slot0, slots):
    left_ref, _, turn_ref, _, _, _, kept_ref = bufs

    def step(slot, t, side, s):
        u, yl, m = ([left_ref[slot, first + k] for k in range(3)] for first in (3, 6, 9))
        right = [turn_ref[side, s, k] for k in range(6)]
        kept = [kept_ref[slot, t, k] for k in range(KEPT)]
        dd = [right[k] - yl[k] for k in range(3)]
        Gd, Gu, Gv = apply_pairs(kept[0:3], u, kept[3:6], dd, m, right[3:6], kept[6:10], kept[10:20])
        return Gd + Gu, Gd + Gv

    sweep(step, bufs, slot0, slots, UNROLL_SECOND, 6, 6)


def finish(left, right, left_curve, right_curve, ml, nr):
    blank = jnp.zeros((2, LANES), jnp.float32)
    left_out = jnp.concatenate(
        [-left[k] for k in range(3)] + [left[3 + k] - left_curve * ml[k] for k in range(3)] + [blank],
        axis=0,
    )
    right_out = jnp.concatenate(
        right[0:3] + [right[3 + k] - right_curve * nr[k] for k in range(3)] + [blank],
        axis=0,
    )
    return left_out, right_out


def first_product(bufs, slot0, tiles, shifts, curves, own):
    for k, (left, right) in enumerate(tiles):
        place_tile(slot0 + k, left, right, shifts[k], bufs)
    first_sweep(bufs, slot0, len(tiles), own)
    out = []
    for k, (left, right) in enumerate(tiles):
        sl, sr = collect(slot0 + k, bufs, LANES // CHUNK // UNROLL_FIRST, 7)
        curves[slot0 + k, 0:1, :] = sl[6]
        curves[slot0 + k, 1:2, :] = sr[6]
        out.append(finish(sl, sr, sl[6], sr[6], left[3], right[3]))
    return out


def second_product(bufs, slot0, tiles, curves):
    for k, (left, right) in enumerate(tiles):
        place_tile(slot0 + k, left, right, None, bufs)
    second_sweep(bufs, slot0, len(tiles))
    out = []
    for k, (left, right) in enumerate(tiles):
        sl, sr = collect(slot0 + k, bufs, LANES // CHUNK // UNROLL_SECOND, 6)
        at = slot0 + k
        out.append(finish(sl, sr, curves[at, 0:1, :], curves[at, 1:2, :], left[3], right[3]))
    return out


def triple_of(x, z):
    F = jnp.sum(x * x, axis=0, keepdims=True)
    some = F > 0.0
    a = jnp.where(some, jnp.sum(x * z, axis=0, keepdims=True) / jnp.where(some, F, 1.0), 0.0)
    rest = z - a * x
    return F, a, jnp.sum(rest * rest, axis=0, keepdims=True)


def merge_triples(F, a, R, axis):
    total = jnp.sum(F, axis=axis, keepdims=True)
    some = total > 0.0
    mean = jnp.where(some, jnp.sum(F * a, axis=axis, keepdims=True) / jnp.where(some, total, 1.0), 0.0)
    gap = a - mean
    return total, mean, jnp.sum(R + F * (gap * gap), axis=axis, keepdims=True)


def pack_triple(triple):
    return jnp.concatenate(list(triple) + [jnp.zeros((5, LANES), jnp.float32)], axis=0)


def unpack_triples(block):
    return block[:, 0, :], block[:, 1, :], block[:, 2, :]


def kernel(
    n_row, n_col,
    frame_ref, start_ref, list_ref, count_ref,
    coef_ref, mode_ref,
    row_frames, col_frames, row_starts, col_starts, row_images, col_images,
    row_in, col_in, row_in2, col_in2, row_out, col_out,
    tri_row, tri_col, tri_row2, tri_col2, tri_buf,
    image_buf, curves, left_ref, right_ref, turn_ref, raw_ref, left_sums, right_sums, kept_ref,
    send_sem, recv_sem,
):
    entries = list_ref.shape[0]
    bufs = (left_ref, right_ref, turn_ref, raw_ref, left_sums, right_sums, kept_ref)
    r = lax.axis_index("row")
    c = lax.axis_index("col")
    total_entries = float(6 * LANES * n_row * n_col)
    zero3 = (0.0, 0.0, 0.0)

    def peer_col(k):
        return lax.rem(c + k, n_col)

    def peer_row(k):
        return lax.rem(r + k, n_row)

    def send(src, dst, phase, lane, device):
        pltpu.make_async_remote_copy(
            src_ref=src,
            dst_ref=dst,
            send_sem=send_sem.at[phase, lane],
            recv_sem=recv_sem.at[phase, lane],
            device_id=device,
            device_id_type=MESH,
        ).start()

    def all_wait(buf, n, sem):
        view = buf.at[pl.ds(0, n - 1)]
        pltpu.make_async_copy(view, view, sem).wait()

    barrier = pltpu.get_barrier_semaphore()

    @pl.loop(1, n_col)
    def _(k):
        pl.semaphore_signal(barrier, inc=1, device_id={"col": peer_col(k)}, device_id_type=MESH)

    @pl.loop(1, n_row)
    def _(k):
        pl.semaphore_signal(barrier, inc=1, device_id={"row": peer_row(k)}, device_id_type=MESH)

    frame = frame_ref[...]
    start = start_ref[...]
    mine = rows_of(frame, start)
    ((own1, own2),) = first_product(bufs, entries, [(mine, mine)], [zero3], curves, True)
    own_first = own1 + own2

    pl.semaphore_wait(barrier, n_row + n_col - 2)

    def spread(row_src, row_buf, col_src, col_buf, phase):
        @pl.loop(1, n_col)
        def _(k):
            send(row_src, row_buf.at[c], phase, 0, {"col": peer_col(k)})

        @pl.loop(1, n_row)
        def _(k):
            send(col_src, col_buf.at[r], phase, 1, {"row": peer_row(k)})

    spread(frame_ref, row_frames, frame_ref, col_frames, 0)
    spread(start_ref, row_starts, start_ref, col_starts, 1)
    row_frames[c] = frame
    col_frames[r] = frame
    row_starts[c] = start
    col_starts[r] = start
    all_wait(row_frames, n_col, recv_sem.at[0, 0])
    all_wait(col_frames, n_row, recv_sem.at[0, 1])
    all_wait(row_starts, n_col, recv_sem.at[1, 0])
    all_wait(col_starts, n_row, recv_sem.at[1, 1])

    period = (5.0, 5.0, 3.5 * (LANES // 16))

    def entry_rows(k, row_vectors, col_vectors):
        a = list_ref[k, 0]
        b = list_ref[k, 1]
        left = rows_of(row_frames[a], row_vectors[a])
        right = rows_of(col_frames[b], col_vectors[b])
        return left, right

    tiles = [entry_rows(k, row_starts, col_starts) for k in range(entries)]
    shifts = [
        [list_ref[k, 2 + x].astype(jnp.float32) * period[x] for x in range(3)] for k in range(entries)
    ]
    outs = first_product(bufs, 0, tiles, shifts, curves, False)

    used = count_ref[0, 0]

    def scatter(row_buf, col_buf, phase, own, outs):
        lefts = [jnp.where(k < used, outs[k][0], 0.0) for k in range(entries)]
        rights = [jnp.where(k < used, outs[k][1], 0.0) for k in range(entries)]

        @pl.loop(0, n_col)
        def _(t):
            acc = jnp.zeros((8, LANES), jnp.float32)
            for k in range(entries):
                acc = acc + jnp.where(list_ref[k, 0] == t, lefts[k], 0.0)
            row_out[phase, t] = acc

        @pl.loop(0, n_row)
        def _(t):
            acc = jnp.zeros((8, LANES), jnp.float32)
            for k in range(entries):
                acc = acc + jnp.where(list_ref[k, 1] == t, rights[k], 0.0)
            col_out[phase, t] = acc

        @pl.loop(1, n_col)
        def _(k):
            t = peer_col(k)
            send(row_out.at[phase, t], row_buf.at[c], 2 + phase, 0, {"col": t})

        @pl.loop(1, n_row)
        def _(k):
            t = peer_row(k)
            send(col_out.at[phase, t], col_buf.at[r], 2 + phase, 1, {"row": t})

        row_buf[c] = row_out[phase, c]
        col_buf[r] = col_out[phase, r]
        all_wait(row_buf, n_col, recv_sem.at[2 + phase, 0])
        all_wait(col_buf, n_row, recv_sem.at[2 + phase, 1])
        total = own + jnp.sum(row_buf[...], axis=0) + jnp.sum(col_buf[...], axis=0)
        u = [frame[3 + k : 4 + k, :] for k in range(3)]
        twist = cross3(u, [total[3 + k : 4 + k, :] for k in range(3)])
        return jnp.concatenate([total[0:3, :]] + list(twist), axis=0)

    image = scatter(row_in, col_in, 0, own_first, outs)

    image_buf[...] = image
    spread(image_buf, row_images, image_buf, col_images, 4)
    row_images[c] = image
    col_images[r] = image

    def scalars_out(triple, slot, buf, phase):
        tri_buf[slot] = pack_triple(triple)

        @pl.loop(1, n_row)
        def _(k):
            send(tri_buf.at[slot], buf.at[r], phase, 1, {"row": peer_row(k)})

        buf[r] = tri_buf[slot]

    def scalars_across(buf, slot, buf2, phase):
        all_wait(buf, n_row, recv_sem.at[phase, 1])
        triple = merge_triples(*unpack_triples(buf[...]), 0)
        tri_buf[slot] = pack_triple(triple)

        @pl.loop(1, n_col)
        def _(k):
            send(tri_buf.at[slot], buf2.at[c], phase, 0, {"col": peer_col(k)})

        buf2[c] = tri_buf[slot]

    def scalars_in(buf2, phase):
        all_wait(buf2, n_col, recv_sem.at[phase, 0])
        triple = merge_triples(*unpack_triples(buf2[...]), 0)
        return merge_triples(*triple, 1)

    scalars_out(triple_of(start, image), 0, tri_row, 5)

    mine = rows_of(frame, image)
    ((own1, own2),) = second_product(bufs, entries, [(mine, mine)], curves)
    own_second = own1 + own2

    scalars_across(tri_row, 1, tri_col, 5)
    all_wait(row_images, n_col, recv_sem.at[4, 0])
    all_wait(col_images, n_row, recv_sem.at[4, 1])

    tiles = [entry_rows(k, row_images, col_images) for k in range(entries)]
    outs = second_product(bufs, 0, tiles, curves)

    image2 = scatter(row_in2, col_in2, 1, own_second, outs)

    F, a, R = scalars_in(tri_col, 5)
    inv_n0 = lax.rsqrt(F / total_entries + norm_eps)
    alpha1 = (a * F) * (inv_n0 * inv_n0) / total_entries
    gap = a - alpha1
    beta1 = jnp.sqrt((R + gap * gap * F) * (inv_n0 * inv_n0) / total_entries + norm_eps)
    scale = inv_n0 / beta1
    second = (image - alpha1 * start) * scale
    image3 = (image2 - alpha1 * image) * scale - (beta1 * inv_n0) * start

    scalars_out(triple_of(second, image3), 2, tri_row2, 6)
    scalars_across(tri_row2, 3, tri_col2, 6)
    F, a, R = scalars_in(tri_col2, 6)
    alpha2 = (a * F) / total_entries
    gap = a - alpha2
    beta2 = jnp.sqrt((R + gap * gap * F) / total_entries + norm_eps)
    mode_ref[...] = (image3 - alpha2 * second) / beta2
    coef_ref[0] = alpha1[0, 0]
    coef_ref[1] = beta1[0, 0]
    coef_ref[2] = alpha2[0, 0]
    coef_ref[3] = beta2[0, 0]

    for phase, row_buf, col_buf in (
        (0, row_frames, col_frames),
        (1, row_starts, col_starts),
        (2, row_in, col_in),
        (3, row_in2, col_in2),
        (4, row_images, col_images),
        (5, tri_col, tri_row),
        (6, tri_col2, tri_row2),
    ):
        all_wait(row_buf, n_col, send_sem.at[phase, 0])
        all_wait(col_buf, n_row, send_sem.at[phase, 1])


def solution(mesh):
    n_row, n_col = mesh.shape["row"], mesh.shape["col"]

    def local(config, start, tile_list, tile_count):
        entries = tile_list.shape[2]
        f32 = jnp.float32
        unroll = max(UNROLL_FIRST, UNROLL_SECOND)

        def vm(*shape):
            return pltpu.VMEM(shape, f32)

        scratch = [
            vm(n_col, 6, LANES), vm(n_row, 6, LANES),
            vm(n_col, 6, LANES), vm(n_row, 6, LANES),
            vm(n_col, 6, LANES), vm(n_row, 6, LANES),
            vm(n_col, 8, LANES), vm(n_row, 8, LANES),
            vm(n_col, 8, LANES), vm(n_row, 8, LANES),
            vm(2, n_col, 8, LANES), vm(2, n_row, 8, LANES),
            vm(n_row, 8, LANES), vm(n_col, 8, LANES),
            vm(n_row, 8, LANES), vm(n_col, 8, LANES),
            vm(4, 8, LANES),
            vm(6, LANES),
            vm(entries + 1, 8, LANES),
            vm(entries + 1, 12, CHUNK, LANES), vm(entries + 1, 12, CHUNK, LANES),
            vm(2, unroll, 12, CHUNK, LANES), vm(2, unroll, 7, CHUNK, LANES),
            vm(entries + 1, LANES // CHUNK, 7, CHUNK, LANES), vm(entries + 1, LANES // CHUNK, 7, CHUNK, LANES),
            vm(entries + 1, LANES // CHUNK, KEPT, CHUNK, LANES),
            pltpu.SemaphoreType.DMA((7, 2)),
            pltpu.SemaphoreType.DMA((7, 2)),
        ]
        return pl.pallas_call(
            functools.partial(kernel, n_row, n_col),
            out_shape=(
                jax.ShapeDtypeStruct((4,), f32),
                jax.ShapeDtypeStruct((6, LANES), f32),
            ),
            in_specs=[
                pl.BlockSpec(memory_space=pltpu.VMEM),
                pl.BlockSpec(memory_space=pltpu.VMEM),
                pl.BlockSpec(memory_space=pltpu.SMEM),
                pl.BlockSpec(memory_space=pltpu.SMEM),
            ],
            out_specs=(
                pl.BlockSpec(memory_space=pltpu.SMEM),
                pl.BlockSpec(memory_space=pltpu.VMEM),
            ),
            scratch_shapes=scratch,
            compiler_params=pltpu.CompilerParams(collective_id=0, has_side_effects=True),
        )(config, start, tile_list.reshape(entries, 5), tile_count)

    placed = (
        P(None, ("row", "col")),
        P(None, ("row", "col")),
        P("row", "col", None, None),
        P("row", "col"),
    )
    return jax.shard_map(
        local, mesh=mesh, in_specs=placed, out_specs=(P(), P(None, ("row", "col"))), check_vma=False
    )
```

```python
import functools
import math

import jax
import jax.numpy as jnp
from jax import lax
from jax.experimental import pallas as pl
from jax.experimental.pallas import tpu as pltpu
from jax.sharding import PartitionSpec as P

MESH = pl.DeviceIdType.MESH
chi_shape = 0.8
chi_energy = (math.sqrt(5.0) - 1.0) / (math.sqrt(5.0) + 1.0)
well_depth = 0.005
cutoff_sq = 20.25
norm_eps = 1e-06
LANES = 128
CHUNK = 8
KEPT = 20
UNROLL_FIRST = 4
UNROLL_SECOND = 4


def dot3(a, b):
    return a[0] * b[0] + a[1] * b[1] + a[2] * b[2]


def cross3(a, b):
    return (
        a[1] * b[2] - a[2] * b[1],
        a[2] * b[0] - a[0] * b[2],
        a[0] * b[1] - a[1] * b[0],
    )


def anisotropy(x, spread, tau, A, B, c, norm, twice_cab, prod_tau):
    t = (2.0 * x) * spread * tau
    h = 0.5 * t * (norm - x * twice_cab)
    xc = x * c
    gA = t * (xc * B - A)
    gB = t * (xc * A - B)
    e = (2.0 * x * x) * spread
    gc = e * (prod_tau - c * h)
    gAB = xc * t
    gAc = e * (c * gA + B * tau)
    gBc = e * (c * gB + A * tau)
    gcc = e * (2.0 * c * gc - h)
    tau2 = 2.0 * tau
    gx = tau2 * h
    first = (gx, gA, gB, gc)
    second = {
        (0, 0): -2.0 * tau2 * gx,
        (0, 1): -tau2 * gA,
        (0, 2): -tau2 * gB,
        (0, 3): -tau2 * gc,
        (1, 1): -t,
        (1, 2): gAB,
        (1, 3): gAc,
        (2, 2): -t,
        (2, 3): gBc,
        (3, 3): gcc,
    }
    return 1.0 - h, first, second


PAIRS = [(p, q) for p in range(4) for q in range(p, 4)]


def derivatives(rho, A, B, c):
    kappa = 1.0 / cutoff_sq
    inv_r = lax.rsqrt(rho)
    tau = inv_r * inv_r
    cc = c * c
    e1 = lax.rsqrt(1.0 - (chi_shape * chi_shape) * cc)
    D1 = e1 * e1
    D2 = 1.0 / (1.0 - (chi_energy * chi_energy) * cc)
    AB = A * B
    norm = A * A + B * B
    twice_cab = 2.0 * c * AB
    prod_tau = AB * tau
    g, g1, g2 = anisotropy(chi_shape, D1, tau, A, B, c, norm, twice_cab, prod_tau)
    q, q1, q2 = anisotropy(chi_energy, D2, tau, A, B, c, norm, twice_cab, prod_tau)
    sigma = lax.rsqrt(g)
    root_g = g * sigma
    alpha = 0.5 * sigma * sigma * sigma
    s = 1.0 / (rho * inv_r - sigma + 1.0)
    s2 = s * s
    s6 = s2 * s2 * s2
    p = jnp.maximum(1.0 - kappa * rho, 0.0)
    inv_p = jnp.where(p > 0.0, 1.0 / p, 0.0)
    weight = (4.0 * well_depth) * e1 * (q * q) * (p * p * p) * s6
    w0 = weight * (s6 - 1.0)
    w1 = weight * s * (6.0 - 12.0 * s6)
    w2 = weight * s2 * (156.0 * s6 - 42.0)
    twice_inv_q = 2.0 / q
    L = [twice_inv_q * f for f in q1]
    lP = (-6.0 * kappa) * inv_p
    lK = (chi_shape * chi_shape) * c * D1
    lKK = (chi_shape * chi_shape) * D1 * (2.0 * D1 - 1.0)
    l = [L[0] + lP, L[1], L[2], L[3] + lK]
    G = [alpha * f for f in g1]
    R = [G[0] + inv_r, G[1], G[2], G[3]]
    up = [w0 * l[k] + w1 * R[k] for k in range(4)]
    tp = [w1 * l[k] + w2 * R[k] for k in range(4)]
    w0h = 0.5 * w0
    w1b = (3.0 * root_g) * w1
    upp = [up[k] - w0h * L[k] for k in range(4)]
    tpp = [tp[k] - w1b * G[k] for k in range(4)]
    w1a = w1 * alpha
    w0q = w0 * twice_inv_q
    out = []
    for a, b in PAIRS:
        value = (upp[a] * L[b] + tpp[a] * G[b]) + (w0q * q2[(a, b)] + w1a * g2[(a, b)])
        if b == 3:
            value = value + up[a] * lK
        if (a, b) == (0, 0):
            value = value + (up[0] - w0 * lP * (1.0 / 3.0)) * lP + (tp[0] - w1 * tau) * inv_r
        if (a, b) == (3, 3):
            value = value + w0 * lKK
        out.append(value)
    return up, out


def apply_pairs(d, u, v, dd, m, n, F, FF):
    S = dict(zip(PAIRS, FF))
    delta = (
        dot3(d, dd),
        dot3(u, dd) + dot3(d, m),
        dot3(v, dd) + dot3(d, n),
        dot3(v, m) + dot3(u, n),
    )
    dF = []
    for p in range(4):
        terms = [S[(min(p, q), max(p, q))] * delta[q] for q in range(4)]
        dF.append((terms[0] + terms[1]) + (terms[2] + terms[3]))
    Gd, Gu, Gv = [], [], []
    for k in range(3):
        Gd.append(
            (dF[0] * d[k] + F[0] * dd[k])
            + (dF[1] * u[k] + F[1] * m[k])
            + (dF[2] * v[k] + F[2] * n[k])
        )
        Gu.append((dF[1] * d[k] + F[1] * dd[k]) + (dF[3] * v[k] + F[3] * n[k]))
        Gv.append((dF[2] * d[k] + F[2] * dd[k]) + (dF[3] * u[k] + F[3] * m[k]))
    return Gd, Gu, Gv


def full(row):
    return jnp.broadcast_to(row, (CHUNK, LANES))


def skew(row):
    return pltpu.roll(full(row), 0, 1, stride=1, stride_axis=0)


def unskew_sums(blocks):
    for rows in (4, 2, 1):
        turned = [pltpu.roll(a[rows : 2 * rows, :], LANES - rows, 1) for a in blocks]
        blocks = [a[0:rows, :] + b for a, b in zip(blocks, turned)]
    return blocks


def rows_of(frame, vector):
    c = [frame[k : k + 1, :] for k in range(3)]
    u = [frame[3 + k : 4 + k, :] for k in range(3)]
    y = [vector[k : k + 1, :] for k in range(3)]
    w = [vector[3 + k : 4 + k, :] for k in range(3)]
    return c, u, y, list(cross3(w, u))


def place_tile(slot, left, right, shift, bufs):
    left_ref, right_ref = bufs[0], bufs[1]
    cl, ul, yl, ml = left
    cr, ur, yr, nr = right
    if shift is not None:
        for k in range(3):
            left_ref[slot, k] = full(cl[k])
            left_ref[slot, 3 + k] = full(ul[k])
            right_ref[slot, 6 + k] = skew(cr[k] + shift[k])
            right_ref[slot, 9 + k] = skew(ur[k])
    for k in range(3):
        left_ref[slot, 6 + k] = full(yl[k])
        left_ref[slot, 9 + k] = full(ml[k])
        right_ref[slot, k] = skew(yr[k])
        right_ref[slot, 3 + k] = skew(nr[k])


def sweep(step, bufs, slot0, slots, unroll, turned, width):
    _, right_ref, turn_ref, raw_ref, left_sums, right_sums, _ = bufs
    chunks = LANES // CHUNK
    groups = chunks // unroll

    def turn_rows(trip):
        slot = slot0 + trip // groups
        side = lax.rem(trip, 2)
        for s in range(unroll):
            by = (lax.rem(trip, groups) * unroll + s) * CHUNK
            for k in range(turned):
                turn_ref[side, s, k] = pltpu.roll(right_ref[slot, k], by, 1)

    def turn_back(trip):
        slot = slot0 + trip // groups
        group = lax.rem(trip, groups)
        side = lax.rem(trip, 2)
        for k in range(width):
            total = None
            for s in range(unroll):
                by = lax.rem(LANES - (group * unroll + s) * CHUNK, LANES)
                part = pltpu.roll(raw_ref[side, s, k], by, 1)
                total = part if total is None else total + part
            right_sums[slot, group, k] = total

    def body(trip):
        slot = slot0 + trip // groups
        group = lax.rem(trip, groups)
        side = lax.rem(trip, 2)
        sums = None
        for s in range(unroll):
            left_terms, right_terms = step(slot, group * unroll + s, side, s)
            for k in range(width):
                raw_ref[side, s, k] = right_terms[k]
            sums = left_terms if sums is None else [a + b for a, b in zip(sums, left_terms)]
        for k in range(width):
            left_sums[slot, group, k] = sums[k]

    trips = slots * groups
    turn_rows(0)

    def first(trip, carry):
        turn_rows(trip + 1)
        body(trip)
        return carry

    def later(trip, carry):
        turn_back(trip - 1)
        turn_rows(trip + 1)
        body(trip)
        return carry

    first(0, 0)
    lax.fori_loop(1, trips - 1, later, 0)
    turn_back(trips - 2)
    body(trips - 1)
    turn_back(trips - 1)


def collect(slot0, slots, bufs, groups, width):
    left_sums, right_sums = bufs[4], bufs[5]

    def joined(ref):
        out = []
        for slot in range(slot0, slot0 + slots):
            for k in range(width):
                parts = [ref[slot, g, k] for g in range(groups)]
                while len(parts) > 1:
                    parts = [a + b for a, b in zip(parts[0::2], parts[1::2])]
                out.append(parts[0])
        return out

    right = unskew_sums(joined(right_sums))
    left = [jnp.sum(a, axis=0, keepdims=True) for a in joined(left_sums)]
    cut = lambda rows: [rows[k * width : (k + 1) * width] for k in range(slots)]
    return list(zip(cut(left), cut(right)))


def first_sweep(bufs, slot0, slots, own):
    left_ref, _, turn_ref, _, _, _, kept_ref = bufs
    lane = lax.broadcasted_iota(jnp.int32, (CHUNK, LANES), 1)
    sub = lax.broadcasted_iota(jnp.int32, (CHUNK, LANES), 0)

    def step(slot, t, side, s):
        left = [left_ref[slot, k] for k in range(12)]
        right = [turn_ref[side, s, k] for k in range(12)]
        d = [right[6 + k] - left[k] for k in range(3)]
        u, v = left[3:6], right[9:12]
        dd = [right[k] - left[6 + k] for k in range(3)]
        m, n = left[9:12], right[3:6]
        if own:
            gap = sub + t * CHUNK
            d[2] = d[2] + jnp.where(gap == 0, 8.0, 0.0)
        A, B, c = dot3(d, u), dot3(d, v), dot3(u, v)
        F, FF = derivatives(dot3(d, d), A, B, c)
        if own:
            once = (gap > 0) & (lane >= gap)
            F = [jnp.where(once, f, 0.0) for f in F]
            FF = [jnp.where(once, f, 0.0) for f in FF]
        for k, value in enumerate(d + v + F + FF):
            kept_ref[slot, t, k] = value
        Gd, Gu, Gv = apply_pairs(d, u, v, dd, m, n, F, FF)
        fc = F[3] * c
        return Gd + Gu + [F[1] * A + fc], Gd + Gv + [F[2] * B + fc]

    sweep(step, bufs, slot0, slots, UNROLL_FIRST, 12, 7)


def second_sweep(bufs, slot0, slots):
    left_ref, _, turn_ref, _, _, _, kept_ref = bufs

    def step(slot, t, side, s):
        u, yl, m = ([left_ref[slot, first + k] for k in range(3)] for first in (3, 6, 9))
        right = [turn_ref[side, s, k] for k in range(6)]
        kept = [kept_ref[slot, t, k] for k in range(KEPT)]
        dd = [right[k] - yl[k] for k in range(3)]
        Gd, Gu, Gv = apply_pairs(kept[0:3], u, kept[3:6], dd, m, right[3:6], kept[6:10], kept[10:20])
        return Gd + Gu, Gd + Gv

    sweep(step, bufs, slot0, slots, UNROLL_SECOND, 6, 6)


def finish(left, right, left_curve, right_curve, ml, nr):
    blank = jnp.zeros((2, LANES), jnp.float32)
    left_out = jnp.concatenate(
        [-left[k] for k in range(3)] + [left[3 + k] - left_curve * ml[k] for k in range(3)] + [blank],
        axis=0,
    )
    right_out = jnp.concatenate(
        right[0:3] + [right[3 + k] - right_curve * nr[k] for k in range(3)] + [blank],
        axis=0,
    )
    return left_out, right_out


def first_product(bufs, slot0, tiles, shifts, curves, own):
    for k, (left, right) in enumerate(tiles):
        place_tile(slot0 + k, left, right, shifts[k], bufs)
    first_sweep(bufs, slot0, len(tiles), own)
    out = []
    sums = collect(slot0, len(tiles), bufs, LANES // CHUNK // UNROLL_FIRST, 7)
    for k, (left, right) in enumerate(tiles):
        sl, sr = sums[k]
        curves[slot0 + k, 0:1, :] = sl[6]
        curves[slot0 + k, 1:2, :] = sr[6]
        out.append(finish(sl, sr, sl[6], sr[6], left[3], right[3]))
    return out


def second_product(bufs, slot0, tiles, curves):
    for k, (left, right) in enumerate(tiles):
        place_tile(slot0 + k, left, right, None, bufs)
    second_sweep(bufs, slot0, len(tiles))
    out = []
    sums = collect(slot0, len(tiles), bufs, LANES // CHUNK // UNROLL_SECOND, 6)
    for k, (left, right) in enumerate(tiles):
        sl, sr = sums[k]
        at = slot0 + k
        out.append(finish(sl, sr, curves[at, 0:1, :], curves[at, 1:2, :], left[3], right[3]))
    return out


def triple_of(x, z):
    F = jnp.sum(x * x, axis=0, keepdims=True)
    some = F > 0.0
    a = jnp.where(some, jnp.sum(x * z, axis=0, keepdims=True) / jnp.where(some, F, 1.0), 0.0)
    rest = z - a * x
    return F, a, jnp.sum(rest * rest, axis=0, keepdims=True)


def merge_triples(F, a, R, axis):
    total = jnp.sum(F, axis=axis, keepdims=True)
    some = total > 0.0
    mean = jnp.where(some, jnp.sum(F * a, axis=axis, keepdims=True) / jnp.where(some, total, 1.0), 0.0)
    gap = a - mean
    return total, mean, jnp.sum(R + F * (gap * gap), axis=axis, keepdims=True)


def pack_triple(triple):
    return jnp.concatenate(list(triple), axis=0)


def unpack_triples(block):
    return block[:, 0, :], block[:, 1, :], block[:, 2, :]


def kernel(
    n_row, n_col,
    frame_ref, start_ref, list_ref, count_ref,
    coef_ref, mode_ref,
    row_frames, col_frames, row_images, col_images,
    row_in, col_in, row_in2, col_in2, row_out, col_out,
    tri_row, tri_col, tri_row2, tri_col2, tri_buf,
    pack_buf, image_buf, curves, left_ref, right_ref, turn_ref, raw_ref, left_sums, right_sums, kept_ref,
    send_sem, recv_sem,
):
    entries = list_ref.shape[2]
    entry = [[list_ref[x, 0, k] for x in range(5)] for k in range(entries)]
    bufs = (left_ref, right_ref, turn_ref, raw_ref, left_sums, right_sums, kept_ref)
    r = lax.axis_index("row")
    c = lax.axis_index("col")
    total_entries = float(6 * LANES * n_row * n_col)
    zero3 = (0.0, 0.0, 0.0)

    def peers(n, me, act):
        half = n // 2
        act(lax.rem(me + half, n))
        group = 5 if (half - 1) % 5 == 0 else half - 1

        def some(i, carry):
            for g in range(group):
                step = 1 + i * group + g
                act(lax.rem(me + half + step, n))
                act(lax.rem(me + half - step, n))
            return carry

        if half > 1:
            lax.fori_loop(0, (half - 1) // group, some, 0)

    def col_peers(act):
        peers(n_col, c, act)

    def row_peers(act):
        peers(n_row, r, act)

    def send(src, dst, phase, lane, device):
        pltpu.make_async_remote_copy(
            src_ref=src,
            dst_ref=dst,
            send_sem=send_sem.at[phase, lane],
            recv_sem=recv_sem.at[phase, lane],
            device_id=device,
            device_id_type=MESH,
        ).start()

    def all_wait(buf, n, sem):
        view = buf.at[pl.ds(0, n - 1)]
        pltpu.make_async_copy(view, view, sem).wait()

    barrier = pltpu.get_barrier_semaphore()

    col_peers(lambda t: pl.semaphore_signal(barrier, inc=1, device_id={"col": t}, device_id_type=MESH))
    row_peers(lambda t: pl.semaphore_signal(barrier, inc=1, device_id={"row": t}, device_id_type=MESH))

    frame = frame_ref[...]
    start = start_ref[...]
    packed = jnp.concatenate([frame, start], axis=0)
    pack_buf[...] = packed
    row_frames[c] = packed
    col_frames[r] = packed
    mine = rows_of(frame, start)
    ((own1, own2),) = first_product(bufs, entries, [(mine, mine)], [zero3], curves, True)
    own_first = own1 + own2

    pl.semaphore_wait(barrier, n_row + n_col - 2)

    def spread(src, row_buf, col_buf, phase):
        col_peers(lambda t: send(src, row_buf.at[c], phase, 0, {"col": t}))
        row_peers(lambda t: send(src, col_buf.at[r], phase, 1, {"row": t}))

    spread(pack_buf, row_frames, col_frames, 0)
    all_wait(row_frames, n_col, recv_sem.at[0, 0])
    all_wait(col_frames, n_row, recv_sem.at[0, 1])

    period = (5.0, 5.0, 3.5 * (LANES // 16))

    def entry_rows(k, row_vectors, col_vectors):
        a, b = entry[k][0], entry[k][1]
        left, right = row_frames[a], col_frames[b]
        if row_vectors is None:
            return rows_of(left[0:6, :], left[6:12, :]), rows_of(right[0:6, :], right[6:12, :])
        return rows_of(left[0:6, :], row_vectors[a]), rows_of(right[0:6, :], col_vectors[b])

    tiles = [entry_rows(k, None, None) for k in range(entries)]
    shifts = [[entry[k][2 + x].astype(jnp.float32) * period[x] for x in range(3)] for k in range(entries)]
    outs = first_product(bufs, 0, tiles, shifts, curves, False)

    used = count_ref[0, 0]

    def scatter(row_buf, col_buf, phase, own, outs):
        lefts = [jnp.where(k < used, outs[k][0], 0.0) for k in range(entries)]
        rights = [jnp.where(k < used, outs[k][1], 0.0) for k in range(entries)]

        def spread_over(n, buf, which, blocks):
            group = 8 if n % 8 == 0 else n

            def some(i, carry):
                for g in range(group):
                    t = i * group + g
                    acc = None
                    for k in range(entries):
                        part = jnp.where(entry[k][which] == t, blocks[k], 0.0)
                        acc = part if acc is None else acc + part
                    buf[phase, t] = acc
                return carry

            lax.fori_loop(0, n // group, some, 0)

        spread_over(n_col, row_out, 0, lefts)
        spread_over(n_row, col_out, 1, rights)
        six = pl.ds(0, 6)
        col_peers(lambda t: send(row_out.at[phase, t, six], row_buf.at[c], 2 + phase, 0, {"col": t}))
        row_peers(lambda t: send(col_out.at[phase, t, six], col_buf.at[r], 2 + phase, 1, {"row": t}))
        row_buf[c] = row_out[phase, c, six, :]
        col_buf[r] = col_out[phase, r, six, :]
        all_wait(row_buf, n_col, recv_sem.at[2 + phase, 0])
        all_wait(col_buf, n_row, recv_sem.at[2 + phase, 1])
        total = own[0:6, :] + jnp.sum(row_buf[...], axis=0) + jnp.sum(col_buf[...], axis=0)
        u = [frame[3 + k : 4 + k, :] for k in range(3)]
        twist = cross3(u, [total[3 + k : 4 + k, :] for k in range(3)])
        return jnp.concatenate([total[0:3, :]] + list(twist), axis=0)

    image = scatter(row_in, col_in, 0, own_first, outs)

    image_buf[...] = image
    spread(image_buf, row_images, col_images, 4)
    row_images[c] = image
    col_images[r] = image

    def scalars_out(triple, slot, buf, phase):
        tri_buf[slot] = pack_triple(triple)

        row_peers(lambda t: send(tri_buf.at[slot], buf.at[r], phase, 1, {"row": t}))
        buf[r] = tri_buf[slot]

    def scalars_across(buf, slot, buf2, phase):
        all_wait(buf, n_row, recv_sem.at[phase, 1])
        triple = merge_triples(*unpack_triples(buf[...]), 0)
        tri_buf[slot] = pack_triple(triple)

        col_peers(lambda t: send(tri_buf.at[slot], buf2.at[c], phase, 0, {"col": t}))
        buf2[c] = tri_buf[slot]

    def scalars_in(buf2, phase):
        all_wait(buf2, n_col, recv_sem.at[phase, 0])
        triple = merge_triples(*unpack_triples(buf2[...]), 0)
        return merge_triples(*triple, 1)

    scalars_out(triple_of(start, image), 0, tri_row, 5)

    mine = rows_of(frame, image)
    ((own1, own2),) = second_product(bufs, entries, [(mine, mine)], curves)
    own_second = own1 + own2

    scalars_across(tri_row, 1, tri_col, 5)
    all_wait(row_images, n_col, recv_sem.at[4, 0])
    all_wait(col_images, n_row, recv_sem.at[4, 1])

    tiles = [entry_rows(k, row_images, col_images) for k in range(entries)]
    outs = second_product(bufs, 0, tiles, curves)

    image2 = scatter(row_in2, col_in2, 1, own_second, outs)

    F, a, R = scalars_in(tri_col, 5)
    inv_n0 = lax.rsqrt(F / total_entries + norm_eps)
    alpha1 = (a * F) * (inv_n0 * inv_n0) / total_entries
    gap = a - alpha1
    beta1 = jnp.sqrt((R + gap * gap * F) * (inv_n0 * inv_n0) / total_entries + norm_eps)
    scale = inv_n0 / beta1
    second = (image - alpha1 * start) * scale
    image3 = (image2 - alpha1 * image) * scale - (beta1 * inv_n0) * start

    scalars_out(triple_of(second, image3), 2, tri_row2, 6)
    scalars_across(tri_row2, 3, tri_col2, 6)
    F, a, R = scalars_in(tri_col2, 6)
    alpha2 = (a * F) / total_entries
    gap = a - alpha2
    beta2 = jnp.sqrt((R + gap * gap * F) / total_entries + norm_eps)
    mode_ref[...] = (image3 - alpha2 * second) / beta2
    coef_ref[0] = alpha1[0, 0]
    coef_ref[1] = beta1[0, 0]
    coef_ref[2] = alpha2[0, 0]
    coef_ref[3] = beta2[0, 0]

    for phase, row_buf, col_buf in (
        (0, row_frames, col_frames),
        (2, row_in, col_in),
        (3, row_in2, col_in2),
        (4, row_images, col_images),
        (5, tri_col, tri_row),
        (6, tri_col2, tri_row2),
    ):
        all_wait(row_buf, n_col, send_sem.at[phase, 0])
        all_wait(col_buf, n_row, send_sem.at[phase, 1])


def solution(mesh):
    n_row, n_col = mesh.shape["row"], mesh.shape["col"]

    def local(config, start, tile_list, tile_count):
        entries = tile_list.shape[2]
        f32 = jnp.float32
        unroll = max(UNROLL_FIRST, UNROLL_SECOND)

        def vm(*shape):
            return pltpu.VMEM(shape, f32)

        scratch = [
            vm(n_col, 12, LANES), vm(n_row, 12, LANES),
            vm(n_col, 6, LANES), vm(n_row, 6, LANES),
            vm(n_col, 6, LANES), vm(n_row, 6, LANES),
            vm(n_col, 6, LANES), vm(n_row, 6, LANES),
            vm(2, n_col, 8, LANES), vm(2, n_row, 8, LANES),
            vm(n_row, 3, LANES), vm(n_col, 3, LANES),
            vm(n_row, 3, LANES), vm(n_col, 3, LANES),
            vm(4, 3, LANES),
            vm(12, LANES),
            vm(6, LANES),
            vm(entries + 1, 8, LANES),
            vm(entries + 1, 12, CHUNK, LANES), vm(entries + 1, 12, CHUNK, LANES),
            vm(2, unroll, 12, CHUNK, LANES), vm(2, unroll, 7, CHUNK, LANES),
            vm(entries + 1, LANES // CHUNK, 7, CHUNK, LANES), vm(entries + 1, LANES // CHUNK, 7, CHUNK, LANES),
            vm(entries + 1, LANES // CHUNK, KEPT, CHUNK, LANES),
            pltpu.SemaphoreType.DMA((7, 2)),
            pltpu.SemaphoreType.DMA((7, 2)),
        ]
        return pl.pallas_call(
            functools.partial(kernel, n_row, n_col),
            out_shape=(
                jax.ShapeDtypeStruct((4,), f32),
                jax.ShapeDtypeStruct((6, LANES), f32),
            ),
            in_specs=[
                pl.BlockSpec(memory_space=pltpu.VMEM),
                pl.BlockSpec(memory_space=pltpu.VMEM),
                pl.BlockSpec(memory_space=pltpu.SMEM),
                pl.BlockSpec(memory_space=pltpu.SMEM),
            ],
            out_specs=(
                pl.BlockSpec(memory_space=pltpu.SMEM),
                pl.BlockSpec(memory_space=pltpu.VMEM),
            ),
            scratch_shapes=scratch,
            compiler_params=pltpu.CompilerParams(collective_id=0, has_side_effects=True),
        )(config, start, tile_list.transpose(0, 3, 1, 2).reshape(5, 1, entries), tile_count)

    placed = (
        P(None, ("row", "col")),
        P(None, ("row", "col")),
        P("row", "col", None, None),
        P("row", "col"),
    )
    return jax.shard_map(
        local, mesh=mesh, in_specs=placed, out_specs=(P(), P(None, ("row", "col"))), check_vma=False
    )
```

```python
import functools
import math

import jax
import jax.numpy as jnp
from jax import lax
from jax.experimental import pallas as pl
from jax.experimental.pallas import tpu as pltpu
from jax.sharding import PartitionSpec as P

MESH = pl.DeviceIdType.MESH
chi_shape = 0.8
chi_energy = (math.sqrt(5.0) - 1.0) / (math.sqrt(5.0) + 1.0)
well_depth = 0.005
cutoff_sq = 20.25
norm_eps = 1e-06
LANES = 128
CHUNK = 8
KEPT = 20
UNROLL_FIRST = 4
UNROLL_SECOND = 8


def dot3(a, b):
    return a[0] * b[0] + a[1] * b[1] + a[2] * b[2]


def cross3(a, b):
    return (
        a[1] * b[2] - a[2] * b[1],
        a[2] * b[0] - a[0] * b[2],
        a[0] * b[1] - a[1] * b[0],
    )


def anisotropy(x, spread, tau, A, B, c, norm, twice_cab, prod_tau):
    e = (2.0 * x * x) * spread
    t = (tau * (1.0 / x)) * e
    h = t * (0.5 * norm - (0.5 * x) * twice_cab)
    xc = x * c
    gA = t * (xc * B - A)
    gB = t * (xc * A - B)
    gc = e * (prod_tau - c * h)
    gx = (2.0 * tau) * h
    return h, (gx, gA, gB, gc), t, e


PAIRS = [(p, q) for p in range(4) for q in range(p, 4)]


def derivatives(rho, A, B, c):
    kappa = 1.0 / cutoff_sq
    inv_r = lax.rsqrt(rho)
    tau = inv_r * inv_r
    cc = c * c
    e1 = lax.rsqrt(1.0 - (chi_shape * chi_shape) * cc)
    D1 = e1 * e1
    D2 = 1.0 / (1.0 - (chi_energy * chi_energy) * cc)
    AB = A * B
    norm = A * A + B * B
    twice_cab = 2.0 * c * AB
    prod_tau = AB * tau
    hg, g1, tg, eg = anisotropy(chi_shape, D1, tau, A, B, c, norm, twice_cab, prod_tau)
    hq, q1, tq, eq = anisotropy(chi_energy, D2, tau, A, B, c, norm, twice_cab, prod_tau)
    g, q = 1.0 - hg, 1.0 - hq
    sigma = lax.rsqrt(g)
    root_g = g * sigma
    alpha = 0.5 * sigma * sigma * sigma
    s = 1.0 / (rho * inv_r - sigma + 1.0)
    s2 = s * s
    s6 = s2 * s2 * s2
    p = jnp.maximum(1.0 - kappa * rho, 0.0)
    inv_p = jnp.where(p > 0.0, 1.0 / p, 0.0)
    weight = (4.0 * well_depth) * e1 * (q * q) * (p * p * p) * s6
    w0 = weight * (s6 - 1.0)
    w1 = weight * s * (6.0 - 12.0 * s6)
    w2 = weight * s2 * (156.0 * s6 - 42.0)
    twice_inv_q = 2.0 / q
    L = [twice_inv_q * f for f in q1]
    lP = (-6.0 * kappa) * inv_p
    lK = (chi_shape * chi_shape) * c * D1
    lKK = (chi_shape * chi_shape) * D1 * (2.0 * D1 - 1.0)
    l = [L[0] + lP, L[1], L[2], L[3] + lK]
    G = [alpha * f for f in g1]
    R = [G[0] + inv_r, G[1], G[2], G[3]]
    up = [w0 * l[k] + w1 * R[k] for k in range(4)]
    tp = [w1 * l[k] + w2 * R[k] for k in range(4)]
    w0h = 0.5 * w0
    w1b = (3.0 * root_g) * w1
    upp = [up[k] - w0h * L[k] for k in range(4)]
    tpp = [tp[k] - w1b * G[k] for k in range(4)]
    w1a = w1 * alpha
    w0q = w0 * twice_inv_q
    tau2 = -2.0 * tau
    wtq, wtg = w0q * tq, w1a * tg
    weq, weg = w0q * eq, w1a * eg
    flat = wtq + wtg
    upK = up[3] - w0 * lK
    cw = c * weq, c * weg
    wet = (weq + weg) * tau
    cross = wet * B + (cw[0] * q1[1] + cw[1] * g1[1]), wet * A + (cw[0] * q1[2] + cw[1] * g1[2])
    bent = {
        (0, 0): (2.0 * tau2) * (w0 * L[0] + w1 * G[0]),
        (0, 1): tau2 * up[1],
        (0, 2): tau2 * up[2],
        (0, 3): tau2 * upK,
        (1, 1): -flat,
        (1, 2): c * (chi_energy * wtq + chi_shape * wtg),
        (1, 3): cross[0],
        (2, 2): -flat,
        (2, 3): cross[1],
        (3, 3): 2.0 * (cw[0] * q1[3] + cw[1] * g1[3]) - (weq * hq + weg * hg),
    }
    out = []
    for a, b in PAIRS:
        value = (upp[a] * L[b] + tpp[a] * G[b]) + bent[(a, b)]
        if b == 3:
            value = value + up[a] * lK
        if (a, b) == (0, 0):
            value = value + (up[0] - w0 * lP * (1.0 / 3.0)) * lP + (tp[0] - w1 * tau) * inv_r
        if (a, b) == (3, 3):
            value = value + w0 * lKK
        out.append(value)
    return up, out


def apply_pairs(d, u, v, dd, m, n, F, FF):
    S = dict(zip(PAIRS, FF))
    delta = (
        dot3(d, dd),
        dot3(u, dd) + dot3(d, m),
        dot3(v, dd) + dot3(d, n),
        dot3(v, m) + dot3(u, n),
    )
    dF = []
    for p in range(4):
        terms = [S[(min(p, q), max(p, q))] * delta[q] for q in range(4)]
        dF.append((terms[0] + terms[1]) + (terms[2] + terms[3]))
    Gd, Gu, Gv = [], [], []
    for k in range(3):
        Gd.append(
            (dF[0] * d[k] + F[0] * dd[k])
            + (dF[1] * u[k] + F[1] * m[k])
            + (dF[2] * v[k] + F[2] * n[k])
        )
        Gu.append((dF[1] * d[k] + F[1] * dd[k]) + (dF[3] * v[k] + F[3] * n[k]))
        Gv.append((dF[2] * d[k] + F[2] * dd[k]) + (dF[3] * u[k] + F[3] * m[k]))
    return Gd, Gu, Gv


def full(row):
    return jnp.broadcast_to(row, (CHUNK, LANES))


def skew(row):
    return pltpu.roll(full(row), 0, 1, stride=1, stride_axis=0)


def unskew_sums(blocks):
    for rows in (4, 2, 1):
        turned = [pltpu.roll(a[rows : 2 * rows, :], LANES - rows, 1) for a in blocks]
        blocks = [a[0:rows, :] + b for a, b in zip(blocks, turned)]
    return blocks


def rows_of(frame, vector):
    c = [frame[k : k + 1, :] for k in range(3)]
    u = [frame[3 + k : 4 + k, :] for k in range(3)]
    y = [vector[k : k + 1, :] for k in range(3)]
    w = [vector[3 + k : 4 + k, :] for k in range(3)]
    return c, u, y, list(cross3(w, u))


def place_tile(slot, left, right, shift, bufs):
    left_ref, right_ref = bufs[0], bufs[1]
    cl, ul, yl, ml = left
    cr, ur, yr, nr = right
    if shift is not None:
        for k in range(3):
            left_ref[slot, k] = full(cl[k])
            left_ref[slot, 3 + k] = full(ul[k])
            right_ref[slot, 6 + k] = skew(cr[k] + shift[k])
            right_ref[slot, 9 + k] = skew(ur[k])
    for k in range(3):
        left_ref[slot, 6 + k] = full(yl[k])
        left_ref[slot, 9 + k] = full(ml[k])
        right_ref[slot, k] = skew(yr[k])
        right_ref[slot, 3 + k] = skew(nr[k])


def sweep(step, bufs, slot0, slots, unroll, turned, width):
    _, right_ref, turn_ref, raw_ref, left_sums, right_sums, _ = bufs
    chunks = LANES // CHUNK
    groups = chunks // unroll

    def turn_rows(trip):
        slot = slot0 + trip // groups
        side = lax.rem(trip, 2)
        for s in range(unroll):
            by = (lax.rem(trip, groups) * unroll + s) * CHUNK
            for k in range(turned):
                turn_ref[side, s, k] = pltpu.roll(right_ref[slot, k], by, 1)

    def turn_back(trip):
        slot = slot0 + trip // groups
        group = lax.rem(trip, groups)
        side = lax.rem(trip, 2)
        for k in range(width):
            total = None
            for s in range(unroll):
                by = lax.rem(LANES - (group * unroll + s) * CHUNK, LANES)
                part = pltpu.roll(raw_ref[side, s, k], by, 1)
                total = part if total is None else total + part
            right_sums[slot, group, k] = total

    def body(trip):
        slot = slot0 + trip // groups
        group = lax.rem(trip, groups)
        side = lax.rem(trip, 2)
        sums = None
        for s in range(unroll):
            left_terms, right_terms = step(slot, group * unroll + s, side, s)
            for k in range(width):
                raw_ref[side, s, k] = right_terms[k]
            sums = left_terms if sums is None else [a + b for a, b in zip(sums, left_terms)]
        for k in range(width):
            left_sums[slot, group, k] = sums[k]

    trips = slots * groups
    turn_rows(0)

    def later(trip, carry):
        turn_back(trip - 1)
        body(trip)
        turn_rows(trip + 1)
        return carry

    body(0)
    turn_rows(1)
    lax.fori_loop(1, trips - 1, later, 0)
    turn_back(trips - 2)
    body(trips - 1)
    turn_back(trips - 1)


def collect(slot0, slots, bufs, groups, width):
    left_sums, right_sums = bufs[4], bufs[5]

    def joined(ref):
        out = []
        for slot in range(slot0, slot0 + slots):
            for k in range(width):
                parts = [ref[slot, g, k] for g in range(groups)]
                while len(parts) > 1:
                    parts = [a + b for a, b in zip(parts[0::2], parts[1::2])]
                out.append(parts[0])
        return out

    right = unskew_sums(joined(right_sums))
    left = [jnp.sum(a, axis=0, keepdims=True) for a in joined(left_sums)]
    cut = lambda rows: [rows[k * width : (k + 1) * width] for k in range(slots)]
    return list(zip(cut(left), cut(right)))


def first_sweep(bufs, slot0, slots, own):
    left_ref, _, turn_ref, _, _, _, kept_ref = bufs
    lane = lax.broadcasted_iota(jnp.int32, (CHUNK, LANES), 1)
    sub = lax.broadcasted_iota(jnp.int32, (CHUNK, LANES), 0)

    def step(slot, t, side, s):
        left = [left_ref[slot, k] for k in range(12)]
        right = [turn_ref[side, s, k] for k in range(12)]
        d = [right[6 + k] - left[k] for k in range(3)]
        u, v = left[3:6], right[9:12]
        dd = [right[k] - left[6 + k] for k in range(3)]
        m, n = left[9:12], right[3:6]
        if own:
            gap = sub + t * CHUNK
            d[2] = d[2] + jnp.where(gap == 0, 8.0, 0.0)
        A, B, c = dot3(d, u), dot3(d, v), dot3(u, v)
        F, FF = derivatives(dot3(d, d), A, B, c)
        if own:
            once = (gap > 0) & (lane >= gap)
            F = [jnp.where(once, f, 0.0) for f in F]
            FF = [jnp.where(once, f, 0.0) for f in FF]
        for k, value in enumerate(d + v + F + FF):
            kept_ref[slot, t, k] = value
        Gd, Gu, Gv = apply_pairs(d, u, v, dd, m, n, F, FF)
        fc = F[3] * c
        return Gd + Gu + [F[1] * A + fc], Gd + Gv + [F[2] * B + fc]

    sweep(step, bufs, slot0, slots, UNROLL_FIRST, 12, 7)


def second_sweep(bufs, slot0, slots):
    left_ref, _, turn_ref, _, _, _, kept_ref = bufs

    def step(slot, t, side, s):
        u, yl, m = ([left_ref[slot, first + k] for k in range(3)] for first in (3, 6, 9))
        right = [turn_ref[side, s, k] for k in range(6)]
        kept = [kept_ref[slot, t, k] for k in range(KEPT)]
        dd = [right[k] - yl[k] for k in range(3)]
        Gd, Gu, Gv = apply_pairs(kept[0:3], u, kept[3:6], dd, m, right[3:6], kept[6:10], kept[10:20])
        return Gd + Gu, Gd + Gv

    sweep(step, bufs, slot0, slots, UNROLL_SECOND, 6, 6)


def finish(left, right, left_curve, right_curve, ml, nr):
    blank = jnp.zeros((2, LANES), jnp.float32)
    left_out = jnp.concatenate(
        [-left[k] for k in range(3)] + [left[3 + k] - left_curve * ml[k] for k in range(3)] + [blank],
        axis=0,
    )
    right_out = jnp.concatenate(
        right[0:3] + [right[3 + k] - right_curve * nr[k] for k in range(3)] + [blank],
        axis=0,
    )
    return left_out, right_out


def first_product(bufs, slot0, tiles, shifts, curves, own):
    for k, (left, right) in enumerate(tiles):
        place_tile(slot0 + k, left, right, shifts[k], bufs)
    first_sweep(bufs, slot0, len(tiles), own)
    out = []
    sums = collect(slot0, len(tiles), bufs, LANES // CHUNK // UNROLL_FIRST, 7)
    for k, (left, right) in enumerate(tiles):
        sl, sr = sums[k]
        curves[slot0 + k, 0:1, :] = sl[6]
        curves[slot0 + k, 1:2, :] = sr[6]
        out.append(finish(sl, sr, sl[6], sr[6], left[3], right[3]))
    return out


def second_product(bufs, slot0, tiles, curves):
    for k, (left, right) in enumerate(tiles):
        place_tile(slot0 + k, left, right, None, bufs)
    second_sweep(bufs, slot0, len(tiles))
    out = []
    sums = collect(slot0, len(tiles), bufs, LANES // CHUNK // UNROLL_SECOND, 6)
    for k, (left, right) in enumerate(tiles):
        sl, sr = sums[k]
        at = slot0 + k
        out.append(finish(sl, sr, curves[at, 0:1, :], curves[at, 1:2, :], left[3], right[3]))
    return out


def triple_of(x, z):
    F = jnp.sum(x * x, axis=0, keepdims=True)
    some = F > 0.0
    a = jnp.where(some, jnp.sum(x * z, axis=0, keepdims=True) / jnp.where(some, F, 1.0), 0.0)
    rest = z - a * x
    return F, a, jnp.sum(rest * rest, axis=0, keepdims=True)


def merge_triples(F, a, R, axis):
    total = jnp.sum(F, axis=axis, keepdims=True)
    some = total > 0.0
    mean = jnp.where(some, jnp.sum(F * a, axis=axis, keepdims=True) / jnp.where(some, total, 1.0), 0.0)
    gap = a - mean
    return total, mean, jnp.sum(R + F * (gap * gap), axis=axis, keepdims=True)


def pack_triple(triple):
    return jnp.concatenate(list(triple), axis=0)


def unpack_triples(block):
    return block[:, 0, :], block[:, 1, :], block[:, 2, :]


def kernel(
    n_row, n_col,
    frame_ref, start_ref, list_ref, count_ref,
    out_ref,
    row_frames, col_frames, row_images, col_images,
    row_in, col_in, row_in2, col_in2, row_out, col_out,
    tri_row, tri_col, tri_row2, tri_col2, tri_buf,
    pack_buf, image_buf, curves, left_ref, right_ref, turn_ref, raw_ref, left_sums, right_sums, kept_ref,
    send_sem, recv_sem,
):
    entries = list_ref.shape[2]
    entry = [[list_ref[x, 0, k] for x in range(5)] for k in range(entries)]
    bufs = (left_ref, right_ref, turn_ref, raw_ref, left_sums, right_sums, kept_ref)
    r = lax.axis_index("row")
    c = lax.axis_index("col")
    total_entries = float(6 * LANES * n_row * n_col)
    zero3 = (0.0, 0.0, 0.0)

    def peers(n, me, act):
        half = n // 2
        act(lax.rem(me + half, n))
        group = 5 if (half - 1) % 5 == 0 else half - 1

        def some(i, carry):
            for g in range(group):
                step = 1 + i * group + g
                act(lax.rem(me + half + step, n))
                act(lax.rem(me + half - step, n))
            return carry

        if half > 1:
            lax.fori_loop(0, (half - 1) // group, some, 0)

    def col_peers(act):
        peers(n_col, c, act)

    def row_peers(act):
        peers(n_row, r, act)

    def send(src, dst, phase, lane, device):
        pltpu.make_async_remote_copy(
            src_ref=src,
            dst_ref=dst,
            send_sem=send_sem.at[phase, lane],
            recv_sem=recv_sem.at[phase, lane],
            device_id=device,
            device_id_type=MESH,
        ).start()

    def all_wait(buf, n, sem):
        view = buf.at[pl.ds(0, n - 1)]
        pltpu.make_async_copy(view, view, sem).wait()

    barrier = pltpu.get_barrier_semaphore()

    col_peers(lambda t: pl.semaphore_signal(barrier, inc=1, device_id={"col": t}, device_id_type=MESH))
    row_peers(lambda t: pl.semaphore_signal(barrier, inc=1, device_id={"row": t}, device_id_type=MESH))

    frame = frame_ref[...]
    start = start_ref[...]
    packed = jnp.concatenate([frame, start], axis=0)
    pack_buf[...] = packed
    row_frames[c] = packed
    col_frames[r] = packed
    mine = rows_of(frame, start)
    ((own1, own2),) = first_product(bufs, entries, [(mine, mine)], [zero3], curves, True)
    own_first = own1 + own2

    pl.semaphore_wait(barrier, n_row + n_col - 2)

    def spread(src, row_buf, col_buf, phase):
        col_peers(lambda t: send(src, row_buf.at[c], phase, 0, {"col": t}))
        row_peers(lambda t: send(src, col_buf.at[r], phase, 1, {"row": t}))

    spread(pack_buf, row_frames, col_frames, 0)
    all_wait(row_frames, n_col, recv_sem.at[0, 0])
    all_wait(col_frames, n_row, recv_sem.at[0, 1])

    period = (5.0, 5.0, 3.5 * (LANES // 16))

    def entry_rows(k, row_vectors, col_vectors):
        a, b = entry[k][0], entry[k][1]
        left, right = row_frames[a], col_frames[b]
        if row_vectors is None:
            return rows_of(left[0:6, :], left[6:12, :]), rows_of(right[0:6, :], right[6:12, :])
        return rows_of(left[0:6, :], row_vectors[a]), rows_of(right[0:6, :], col_vectors[b])

    tiles = [entry_rows(k, None, None) for k in range(entries)]
    shifts = [[entry[k][2 + x].astype(jnp.float32) * period[x] for x in range(3)] for k in range(entries)]
    outs = first_product(bufs, 0, tiles, shifts, curves, False)

    used = count_ref[0, 0]

    def scatter(row_buf, col_buf, phase, own, outs, meanwhile):
        lefts = [jnp.where(k < used, outs[k][0], 0.0) for k in range(entries)]
        rights = [jnp.where(k < used, outs[k][1], 0.0) for k in range(entries)]

        def spread_over(n, buf, which, blocks):
            group = 8 if n % 8 == 0 else n

            def some(i, carry):
                for g in range(group):
                    t = i * group + g
                    acc = None
                    for k in range(entries):
                        part = jnp.where(entry[k][which] == t, blocks[k], 0.0)
                        acc = part if acc is None else acc + part
                    buf[phase, t] = acc
                return carry

            lax.fori_loop(0, n // group, some, 0)

        spread_over(n_col, row_out, 0, lefts)
        spread_over(n_row, col_out, 1, rights)
        six = pl.ds(0, 6)
        col_peers(lambda t: send(row_out.at[phase, t, six], row_buf.at[c], 2 + phase, 0, {"col": t}))
        row_peers(lambda t: send(col_out.at[phase, t, six], col_buf.at[r], 2 + phase, 1, {"row": t}))
        row_buf[c] = row_out[phase, c, six, :]
        col_buf[r] = col_out[phase, r, six, :]
        between = meanwhile()
        all_wait(row_buf, n_col, recv_sem.at[2 + phase, 0])
        all_wait(col_buf, n_row, recv_sem.at[2 + phase, 1])
        total = own[0:6, :] + jnp.sum(row_buf[...], axis=0) + jnp.sum(col_buf[...], axis=0)
        u = [frame[3 + k : 4 + k, :] for k in range(3)]
        twist = cross3(u, [total[3 + k : 4 + k, :] for k in range(3)])
        return jnp.concatenate([total[0:3, :]] + list(twist), axis=0), between

    image, _ = scatter(row_in, col_in, 0, own_first, outs, lambda: None)

    image_buf[...] = image
    spread(image_buf, row_images, col_images, 4)
    row_images[c] = image
    col_images[r] = image

    def scalars_out(triple, slot, buf, phase):
        tri_buf[slot] = pack_triple(triple)

        row_peers(lambda t: send(tri_buf.at[slot], buf.at[r], phase, 1, {"row": t}))
        buf[r] = tri_buf[slot]

    def scalars_across(buf, slot, buf2, phase):
        all_wait(buf, n_row, recv_sem.at[phase, 1])
        triple = merge_triples(*unpack_triples(buf[...]), 0)
        tri_buf[slot] = pack_triple(triple)

        col_peers(lambda t: send(tri_buf.at[slot], buf2.at[c], phase, 0, {"col": t}))
        buf2[c] = tri_buf[slot]

    def scalars_in(buf2, phase):
        all_wait(buf2, n_col, recv_sem.at[phase, 0])
        triple = merge_triples(*unpack_triples(buf2[...]), 0)
        return merge_triples(*triple, 1)

    scalars_out(triple_of(start, image), 0, tri_row, 5)

    mine = rows_of(frame, image)
    ((own1, own2),) = second_product(bufs, entries, [(mine, mine)], curves)
    own_second = own1 + own2

    scalars_across(tri_row, 1, tri_col, 5)
    all_wait(row_images, n_col, recv_sem.at[4, 0])
    all_wait(col_images, n_row, recv_sem.at[4, 1])

    tiles = [entry_rows(k, row_images, col_images) for k in range(entries)]
    outs = second_product(bufs, 0, tiles, curves)

    def first_scalars():
        F, a, R = scalars_in(tri_col, 5)
        inv_n0 = lax.rsqrt(F / total_entries + norm_eps)
        alpha1 = (a * F) * (inv_n0 * inv_n0) / total_entries
        gap = a - alpha1
        beta1 = jnp.sqrt((R + gap * gap * F) * (inv_n0 * inv_n0) / total_entries + norm_eps)
        scale = inv_n0 / beta1
        second = (image - alpha1 * start) * scale
        return alpha1, beta1, second, scale, (alpha1 * scale) * image + (beta1 * inv_n0) * start

    image2, (alpha1, beta1, second, scale, less) = scatter(row_in2, col_in2, 1, own_second, outs, first_scalars)
    image3 = image2 * scale - less

    scalars_out(triple_of(second, image3), 2, tri_row2, 6)
    scalars_across(tri_row2, 3, tri_col2, 6)
    F, a, R = scalars_in(tri_col2, 6)
    alpha2 = (a * F) / total_entries
    gap = a - alpha2
    beta2 = jnp.sqrt((R + gap * gap * F) / total_entries + norm_eps)
    lane = lax.broadcasted_iota(jnp.int32, (1, LANES), 1)
    coefs = jnp.where(lane == 0, alpha1, jnp.where(lane == 1, beta1, jnp.where(lane == 2, alpha2, beta2)))
    out_ref[0:6, :] = (image3 - alpha2 * second) / beta2
    out_ref[6:8, :] = jnp.broadcast_to(coefs, (2, LANES))

    for phase, row_buf, col_buf in (
        (0, row_frames, col_frames),
        (2, row_in, col_in),
        (3, row_in2, col_in2),
        (4, row_images, col_images),
        (5, tri_col, tri_row),
        (6, tri_col2, tri_row2),
    ):
        all_wait(row_buf, n_col, send_sem.at[phase, 0])
        all_wait(col_buf, n_row, send_sem.at[phase, 1])


def part_kernel(out_ref, coef_ref, mode_ref):
    mode_ref[...] = out_ref[0:6, :]
    row = out_ref[6:7, :]
    for k in range(4):
        coef_ref[k] = row[0, k]


def solution(mesh):
    n_row, n_col = mesh.shape["row"], mesh.shape["col"]

    def local(config, start, tile_list, tile_count):
        entries = tile_list.shape[2]
        f32 = jnp.float32
        unroll = max(UNROLL_FIRST, UNROLL_SECOND)

        def vm(*shape):
            return pltpu.VMEM(shape, f32)

        scratch = [
            vm(n_col, 12, LANES), vm(n_row, 12, LANES),
            vm(n_col, 6, LANES), vm(n_row, 6, LANES),
            vm(n_col, 6, LANES), vm(n_row, 6, LANES),
            vm(n_col, 6, LANES), vm(n_row, 6, LANES),
            vm(2, n_col, 8, LANES), vm(2, n_row, 8, LANES),
            vm(n_row, 3, LANES), vm(n_col, 3, LANES),
            vm(n_row, 3, LANES), vm(n_col, 3, LANES),
            vm(4, 3, LANES),
            vm(12, LANES),
            vm(6, LANES),
            vm(entries + 1, 8, LANES),
            vm(entries + 1, 12, CHUNK, LANES), vm(entries + 1, 12, CHUNK, LANES),
            vm(2, unroll, 12, CHUNK, LANES), vm(2, unroll, 7, CHUNK, LANES),
            vm(entries + 1, LANES // CHUNK, 7, CHUNK, LANES), vm(entries + 1, LANES // CHUNK, 7, CHUNK, LANES),
            vm(entries + 1, LANES // CHUNK, KEPT, CHUNK, LANES),
            pltpu.SemaphoreType.DMA((7, 2)),
            pltpu.SemaphoreType.DMA((7, 2)),
        ]
        out = pl.pallas_call(
            functools.partial(kernel, n_row, n_col),
            out_shape=jax.ShapeDtypeStruct((8, LANES), f32),
            in_specs=[
                pl.BlockSpec(memory_space=pltpu.VMEM),
                pl.BlockSpec(memory_space=pltpu.VMEM),
                pl.BlockSpec(memory_space=pltpu.SMEM),
                pl.BlockSpec(memory_space=pltpu.SMEM),
            ],
            out_specs=pl.BlockSpec(memory_space=pltpu.VMEM),
            scratch_shapes=scratch,
            compiler_params=pltpu.CompilerParams(collective_id=0, has_side_effects=True),
        )(config, start, tile_list.transpose(0, 3, 1, 2).reshape(5, 1, entries), tile_count)
        return pl.pallas_call(
            part_kernel,
            out_shape=(jax.ShapeDtypeStruct((4,), f32), jax.ShapeDtypeStruct((6, LANES), f32)),
            in_specs=[pl.BlockSpec(memory_space=pltpu.VMEM)],
            out_specs=(pl.BlockSpec(memory_space=pltpu.SMEM), pl.BlockSpec(memory_space=pltpu.VMEM)),
        )(out)

    placed = (
        P(None, ("row", "col")),
        P(None, ("row", "col")),
        P("row", "col", None, None),
        P("row", "col"),
    )
    return jax.shard_map(
        local, mesh=mesh, in_specs=placed, out_specs=(P(), P(None, ("row", "col"))), check_vma=False
    )
```
